32 devices in a mesh: grp: 2 (over y), row: 4 (over z), col: 2 (over x), sub: 2 (over core).
Axes of the slice: x: 2, y: 2, z: 4, core: 2. Of those that a mesh axis runs over, the one named last changes fastest.
Arguments:
- left_features: bfloat16 [256, 256, 128], P(('grp', 'row'), ('col', 'sub')), parts along dimension 0, may hold values from -16 to 16
- right_features: bfloat16 [256, 256, 128], P(('grp', 'row'), ('col', 'sub')), parts along dimension 0, may hold values from -16 to 16
- left_image: float32 [3, 256, 256], P(None, ('grp', 'row'), ('col', 'sub')), parts along dimension 1, may hold values from -4 to 4
- query_key: bfloat16 [128, 128], replicated, may hold values from -0.5 to 0.5
- value_weight: bfloat16 [128, 128], replicated, may hold values from -0.5 to 0.5
- out_weight: bfloat16 [128, 128], replicated, may hold values from -0.5 to 0.5
- occlusion_weight: float32 [128], replicated, may hold values from -0.5 to 0.5
- first_conv: bfloat16 [9, 64, 5], replicated, may hold values from -0.875 to 0.875
- middle_conv: bfloat16 [3, 9, 64, 64], replicated, may hold values from -0.25 to 0.25
- last_conv: bfloat16 [9, 2, 64], replicated, may hold values from -0.25 to 0.25
Outputs:
- disparity_out: float32 [256, 256], P(('grp', 'row'), ('col', 'sub')), parts along dimension 0
- occlusion_out: float32 [256, 256], P(('grp', 'row'), ('col', 'sub')), parts along dimension 0
The draws below stay inside these ranges and needn't reach their ends.
There are 2 independent parts, one for each index of `grp`. The reference program is written for one: setup_inputs(seed, part) draws one part's arguments, and reference() takes and returns one part's arrays. A program takes and returns all parts, laid end to end along the dimension named above; an argument that names none is the same for every part. Nothing has to cross between parts.
All inputs are finite; a program needn't handle non-finite values.
Results may differ from the reference program's by a relative error of at most 0.0033.
Values may be sent and summed in bfloat16 or wider, within the bound.
No kernel may reach another device: no remote copies, remote signals or barrier semaphores. Data moves between devices by JAX's collectives and lax.ppermute only.
A program may use at most 64 MiB of HBM per device.

```python
import jax
import jax.numpy as jnp
from jax import lax

C = 128
HEADS = 8
HEAD = 16
CONV = 64
H = 128
W = 256


def feature_pair(key):
    base = jax.random.fold_in(key, 11)
    streams = jax.random.split(base, 2)
    left = jax.random.truncated_normal(streams[0], -6.0, 6.0, (H, W, C), jnp.float32)
    right = jax.random.truncated_normal(streams[1], -6.0, 6.0, (H, W, C), jnp.float32)
    return (left, right)


def draw_left_features(key, part):
    return feature_pair(key)[0].astype(jnp.bfloat16)


def draw_right_features(key, part):
    return feature_pair(key)[1].astype(jnp.bfloat16)


def block_scale(key, dims, pieces, least, top_value):
    def one(dim, blocks):
        steps = jax.random.uniform(jax.random.fold_in(jax.random.fold_in(key, 6), dim), (blocks,), jnp.float32, least / len(pieces), top_value / len(pieces))
        return jnp.repeat(jnp.exp(steps), dims[dim] // blocks).reshape((-1,) + (1,) * (len(dims) - dim - 1))

    factor_of = one(*pieces[0])
    for cut in pieces[1:]:
        factor_of = factor_of * one(*cut)
    return factor_of


def noise(rng, dims, scale, reach, cuts=(), kind=jnp.bfloat16):
    result = scale * jax.random.normal(rng, dims, jnp.float32)
    if cuts:
        result = result * block_scale(rng, dims, cuts, -0.22, 0.18)
    return jnp.clip(result, -reach, reach).astype(kind)


def setup_inputs(seed: int = 0, part: int = 0) -> dict:
    arg_keys = jax.random.split(jax.random.key(seed), 11)
    part_splits = jax.random.split(jax.random.fold_in(arg_keys[10], part), 11)
    return {
        "left_features": draw_left_features(jax.random.fold_in(jax.random.fold_in(arg_keys[10], part), 71), part),
        "right_features": draw_right_features(jax.random.fold_in(jax.random.fold_in(arg_keys[10], part), 71), part),
        "left_image": noise(part_splits[2], (3, H, W), 1.0, 4.0, ((1, 4), (2, 4)), jnp.float32),
        "query_key": noise(arg_keys[3], (C, C), C ** -0.5, 0.5),
        "value_weight": noise(arg_keys[4], (C, C), C ** -0.5, 0.5),
        "out_weight": noise(arg_keys[5], (C, C), C ** -0.5, 0.5),
        "occlusion_weight": noise(arg_keys[6], (C,), C ** -0.5, 0.5, (), jnp.float32),
        "first_conv": noise(arg_keys[7], (9, CONV, 5), 45 ** -0.5, 0.875),
        "middle_conv": noise(arg_keys[8], (3, 9, CONV, CONV), (9 * CONV) ** -0.5, 0.25),
        "last_conv": noise(arg_keys[9], (9, 2, CONV), (9 * CONV) ** -0.5, 0.25),
    }


def conv_same(source, weight):
    padded = jnp.pad(source, ((0, 0), (1, 1), (1, 1))).astype(jnp.float32)
    height = source.shape[1]
    across = source.shape[2]
    summed = jnp.zeros((weight.shape[1], height, across), jnp.float32)
    for offset in range(9):
        window = padded[:, offset // 3:offset // 3 + height, offset % 3:offset % 3 + across]
        summed = summed + jnp.einsum('oc,crw->orw', weight[offset].astype(jnp.float32), window)
    return summed

def reference(left_features, right_features, left_image, query_key, value_weight, out_weight, occlusion_weight, first_conv, middle_conv, last_conv):
    scaling = HEAD ** (-0.5)
    left_wide = left_features.astype(jnp.float32)
    right_wide = right_features.astype(jnp.float32)
    queries = (jnp.einsum('rwc,cd->rwd', left_wide, query_key.astype(jnp.float32)) * scaling).astype(jnp.bfloat16)
    keys = jnp.einsum('rwc,cd->rwd', right_wide, query_key.astype(jnp.float32)).astype(jnp.bfloat16)
    values = jnp.einsum('rwc,cd->rwd', right_wide, value_weight.astype(jnp.float32)).astype(jnp.bfloat16)
    queries = queries.reshape(H, W, HEADS, HEAD)
    keys = keys.reshape(H, W, HEADS, HEAD)
    values = values.reshape(H, W, HEADS, HEAD)
    positions = jnp.arange(W)
    allowed = positions[None, :] <= positions[:, None]
    places = positions.astype(jnp.float32)

    def one_row(inputs):
        query_row, key_row, value_row = inputs
        scores = jnp.einsum('ihd,jhd->hij', query_row.astype(jnp.float32), key_row.astype(jnp.float32))
        scores = jnp.where(allowed[None], scores, -jnp.inf)
        largest = lax.optimization_barrier(jnp.max(scores, axis=-1, keepdims=True))
        exponent = jnp.exp(scores - largest)
        totals = lax.optimization_barrier(jnp.sum(exponent, axis=-1, keepdims=True))
        probabilities = (exponent / totals).astype(jnp.bfloat16)
        blended = jnp.einsum('hij,jhd->ihd', probabilities.astype(jnp.float32), value_row.astype(jnp.float32)).astype(jnp.bfloat16)
        weighted = jnp.einsum('hij,j->hi', exponent, places, precision=lax.Precision.HIGHEST)
        shifts = places[None, :] - weighted / totals[..., 0]
        return (blended, lax.optimization_barrier(jnp.sum(shifts, axis=0)))
    head_out, shift_sums = lax.map(one_row, (queries, keys, values))
    head_out = head_out.reshape(H, W, C)
    disparity = shift_sums * (8.0 / (HEADS * W))
    attended = jnp.einsum('rwc,cd->rwd', head_out.astype(jnp.float32), out_weight.astype(jnp.float32))
    centre = lax.optimization_barrier(jnp.mean(attended, axis=-1, keepdims=True))
    spread = lax.optimization_barrier(jnp.mean((attended - centre) ** 2, axis=-1, keepdims=True))
    normalized = (attended - centre) * lax.rsqrt(spread + 1e-05)
    occlusion = jnp.einsum('rwc,c->rw', normalized, occlusion_weight, precision=lax.Precision.HIGHEST)
    stacked = jnp.concatenate([disparity[None], occlusion[None], left_image], axis=0).astype(jnp.bfloat16)
    layer_one = jax.nn.relu(conv_same(stacked, first_conv)).astype(jnp.bfloat16)
    layer_two = jax.nn.relu(conv_same(layer_one, middle_conv[0])).astype(jnp.bfloat16)
    layer_three = jax.nn.relu(layer_one.astype(jnp.float32) + conv_same(layer_two, middle_conv[1])).astype(jnp.bfloat16)
    layer_four = jax.nn.relu(conv_same(layer_three, middle_conv[2])).astype(jnp.bfloat16)
    correction = conv_same(layer_four, last_conv)
    disparity_out = disparity + correction[0]
    occlusion_out = jax.nn.sigmoid(occlusion + correction[1])
    return (disparity_out, occlusion_out)
```

```python
import functools

import jax
import jax.numpy as jnp
from jax import lax
from jax.experimental import pallas as pl
from jax.experimental.pallas import tpu as pltpu
from jax.sharding import PartitionSpec as P

C = 128
HEADS = 8
HEAD = 16
CONV = 64
RIM = 5
SLOTS = 8
BLOCK = 128
F32 = jnp.float32
BF16 = jnp.bfloat16
GROUP = ("col", "sub")
BANDS = ("row", "col", "sub")


def dot(a, b, dims):
    return lax.dot_general(a, b, (dims, ((), ())), preferred_element_type=F32)


def attention_row(left, right, qw, kw, vw, ow, occ):
    length = left.shape[0]
    blocks = length // BLOCK
    queries = (dot(qw, left, ((1,), (1,))) * (HEAD**-0.5)).astype(BF16)
    keys = dot(right, kw, ((1,), (0,))).astype(BF16)
    values = dot(vw, right, ((1,), (1,))).astype(BF16)

    channel = lax.broadcasted_iota(jnp.int32, (1, C), 1)
    scores = []
    for j in range(blocks):
        part = keys[BLOCK * j : BLOCK * (j + 1)]
        by_head = jnp.concatenate(
            [jnp.where(channel // HEAD == h, part, jnp.zeros_like(part)) for h in range(HEADS)],
            axis=0,
        )
        scores.append(dot(by_head, queries[:, BLOCK * j :], ((1,), (0,))))

    key_at = lax.broadcasted_iota(jnp.int32, (BLOCK, BLOCK), 0)
    query_at = lax.broadcasted_iota(jnp.int32, (BLOCK, BLOCK), 1)
    allowed = key_at <= query_at
    line = lax.broadcasted_iota(jnp.int32, (HEAD, length), 0)
    place = lax.broadcasted_iota(jnp.int32, (HEAD, length), 1)
    counts = jnp.where(
        line == 0,
        1,
        jnp.where(line == 1, place % BLOCK, jnp.where(line == 2, place - place % BLOCK, 0)),
    )
    counts = counts.astype(F32).astype(BF16)

    heads = [[] for _ in range(blocks)]
    means = [jnp.zeros((1, BLOCK), F32) for _ in range(blocks)]
    for h in range(HEADS):
        stacked = jnp.concatenate([values[HEAD * h : HEAD * (h + 1)], counts], axis=0)
        for i in range(blocks):
            parts = []
            for j in range(i + 1):
                piece = scores[j][
                    BLOCK * h : BLOCK * (h + 1), BLOCK * (i - j) : BLOCK * (i - j + 1)
                ]
                if j == i:
                    piece = jnp.where(allowed, piece, -jnp.inf)
                parts.append(piece)
            largest = functools.reduce(
                jnp.maximum, [jnp.max(p, axis=0, keepdims=True) for p in parts]
            )
            expon = jnp.concatenate(
                [jnp.exp(p - largest).astype(BF16) for p in parts], axis=0
            )
            sums = dot(stacked[:, : BLOCK * (i + 1)], expon, ((1,), (0,)))
            inverse = 1.0 / sums[HEAD : HEAD + 1]
            heads[i].append((sums[:HEAD] * inverse).astype(BF16))
            means[i] = means[i] + (sums[HEAD + 1 : HEAD + 2] + sums[HEAD + 2 : HEAD + 3]) * inverse

    head_out = jnp.concatenate([jnp.concatenate(b, axis=0) for b in heads], axis=1)
    mean = jnp.concatenate(means, axis=1)
    column = lax.broadcasted_iota(jnp.int32, (1, length), 1).astype(F32)
    disparity = (HEADS * column - mean) * (8.0 / (HEADS * length))
    attended = dot(ow, head_out, ((1,), (0,)))
    centred = attended - jnp.mean(attended, axis=0, keepdims=True)
    spread = jnp.mean(centred * centred, axis=0, keepdims=True)
    occlusion = jnp.sum(centred * occ, axis=0, keepdims=True) * lax.rsqrt(spread + 1e-05)
    return disparity, occlusion


def attention_kernel(group, at_ref, own_left, own_right, *refs):
    pieces = refs[: group - 1]
    qw, kw, vw, ow, occ, image, stacked_ref, maps_ref, left_s, right_s = refs[group - 1 :]
    tile = own_left.shape[1]
    me = at_ref[0]
    row = pl.program_id(0)
    for k in range(group):
        start = pl.multiple_of((me ^ k) * tile, tile)
        if k == 0:
            left_s[pl.ds(start, tile), :] = own_left[0]
            right_s[pl.ds(start, tile), :] = own_right[0]
        else:
            left_s[pl.ds(start, tile), :] = pieces[k - 1][0, 0]
            right_s[pl.ds(start, tile), :] = pieces[k - 1][1, 0]
    disparity, occlusion = attention_row(
        left_s[...], right_s[...], qw[...], kw[...], vw[...], ow[...], occ[...]
    )
    maps = jnp.concatenate([disparity, occlusion], axis=0)
    maps_ref[row] = maps
    full = jnp.concatenate([maps, jnp.zeros((SLOTS - 2, maps.shape[1]), F32)], axis=0)
    stacked_ref[row] = (full + image[row].astype(F32)).astype(BF16)


def attention(at, left, right, pieces, weights, image, rows, length):
    group = len(pieces) + 1
    tile = left.shape[1]
    own = pl.BlockSpec((1, tile, C), lambda r, at: (at[0] * rows + r, 0, 0))
    piece = pl.BlockSpec((2, 1, tile, C), lambda r, at: (0, r, 0, 0))
    whole = lambda a: pl.BlockSpec(a.shape, lambda r, at, n=a.ndim: (0,) * n)
    return pl.pallas_call(
        functools.partial(attention_kernel, group),
        name="attention",
        out_shape=(
            jax.ShapeDtypeStruct((rows, SLOTS, length), BF16),
            jax.ShapeDtypeStruct((rows, 2, length), F32),
        ),
        grid_spec=pltpu.PrefetchScalarGridSpec(
            num_scalar_prefetch=1,
            grid=(rows,),
            in_specs=[own, own]
            + [piece] * (group - 1)
            + [whole(w) for w in weights]
            + [whole(image)],
            out_specs=(
                pl.BlockSpec((rows, SLOTS, length), lambda r, at: (0, 0, 0)),
                pl.BlockSpec((rows, 2, length), lambda r, at: (0, 0, 0)),
            ),
            scratch_shapes=[pltpu.VMEM((length, C), BF16)] * 2,
        ),
        compiler_params=pltpu.CompilerParams(
            dimension_semantics=("arbitrary",), vmem_limit_bytes=32 << 20
        ),
    )(at, left, right, *pieces, *weights, image)


def spread_taps(x):
    length = x.shape[1]
    column = lax.broadcasted_iota(jnp.int32, (1, length), 1)
    before = jnp.where(column == 0, 0.0, pltpu.roll(x, 1, 1))
    after = jnp.where(column == length - 1, 0.0, pltpu.roll(x, length - 1, 1))
    return before, x, after


def conv_rows(source, weight, outs, count, finish):
    def at(q):
        p = dot(weight[...], source[q], ((1,), (0,)))
        return p[:outs], p[outs : 2 * outs], p[2 * outs :]

    top0, top1, _ = at(0)
    next0, next1, _ = at(1)
    del top1

    def body(r, carry):
        first, second = carry
        p0, p1, p2 = at(r + 2)
        finish(r, first + p2)
        return second + p1, p0

    lax.fori_loop(0, count, body, (top0 + next1, next0))


def conv_kernel(group, hops, at_ref, own, maps, *refs):
    others = refs[: 2 * hops]
    w1, w2, w3, w4, w5 = refs[2 * hops : 2 * hops + 5]
    outs = refs[2 * hops + 5 : 2 * hops + 5 + group]
    x0, x1, x2, x3, x4 = refs[2 * hops + 5 + group :]
    rows, _, length = own.shape
    me, place, last = at_ref[0], at_ref[1], at_ref[2]
    base = place * rows

    def put(q, block):
        before, same, after = spread_taps(block.astype(F32))
        zero = jnp.zeros_like(same)
        x0[q] = jnp.concatenate([before, same, after, zero], axis=0).astype(BF16)

    for q in range(rows):
        put(RIM + q, own[q])
    for d in range(1, hops + 1):
        flag = jnp.bitwise_and(place, d) != 0
        a, b = others[2 * d - 2], others[2 * d - 1]
        for q in range(rows):
            up = RIM - d * rows + q
            if up >= 0:
                put(up, jnp.where(flag, a[q], b[q]))
            down = RIM + d * rows + q
            if down < rows + 2 * RIM:
                put(down, jnp.where(flag, b[q], a[q]))

    def store(target, lead, residual=None):
        def finish(r, total):
            if residual is not None:
                total = total + residual[r + 2, CONV : 2 * CONV].astype(F32)
            g = base + r - lead
            inside = jnp.logical_and(g >= 0, g < last)
            y = jnp.where(inside, jnp.maximum(total, 0.0), 0.0)
            before, same, after = spread_taps(y)
            target[r, :CONV] = before.astype(BF16)
            target[r, CONV : 2 * CONV] = same.astype(BF16)
            target[r, 2 * CONV :] = after.astype(BF16)

        return finish

    conv_rows(x0, w1, CONV, rows + 8, store(x1, 4))
    conv_rows(x1, w2, CONV, rows + 6, store(x2, 3))
    conv_rows(x2, w3, CONV, rows + 4, store(x3, 2, x1))
    conv_rows(x3, w4, CONV, rows + 2, store(x4, 1))

    tile = length // group

    def last_row(r, total):
        m = maps[r]
        disparity = m[:1] + total[:1]
        occlusion = jax.nn.sigmoid(m[1:2] + total[1:2])
        both = jnp.concatenate([disparity, occlusion], axis=0)
        cut = [both[:, tile * c : tile * (c + 1)] for c in range(group)]
        for k in range(group):
            pick = cut[0]
            for c in range(1, group):
                pick = jnp.where((me ^ k) == c, cut[c], pick)
            outs[k][r] = pick

    conv_rows(x4, w5, SLOTS, rows, last_row)


def convolutions(at, own, maps, others, weights, group):
    rows, _, length = own.shape
    tile = length // group
    hops = len(others) // 2
    vmem = pl.BlockSpec(memory_space=pltpu.VMEM)
    depth = 3 * CONV
    return pl.pallas_call(
        functools.partial(conv_kernel, group, hops),
        name="convolutions",
        out_shape=[jax.ShapeDtypeStruct((rows, 2, tile), F32)] * group,
        in_specs=[pl.BlockSpec(memory_space=pltpu.SMEM)]
        + [vmem] * (2 + len(others) + len(weights)),
        out_specs=[vmem] * group,
        scratch_shapes=[
            pltpu.VMEM((rows + 10, 4 * SLOTS, length), BF16),
            pltpu.VMEM((rows + 8, depth, length), BF16),
            pltpu.VMEM((rows + 6, depth, length), BF16),
            pltpu.VMEM((rows + 4, depth, length), BF16),
            pltpu.VMEM((rows + 2, depth, length), BF16),
        ],
        compiler_params=pltpu.CompilerParams(vmem_limit_bytes=40 << 20),
    )(at, own, maps, *others, *weights)


def place_kernel(group, at_ref, *refs):
    pieces, (first, second) = refs[:group], refs[group:]
    rows = pieces[0].shape[0]
    me = at_ref[0]
    for k in range(group):
        start = (me ^ k) * rows
        for r in range(rows):
            first[pl.ds(start + r, 1), :] = pieces[k][r, 0:1]
            second[pl.ds(start + r, 1), :] = pieces[k][r, 1:2]


def place_rows(at, pieces):
    group = len(pieces)
    rows, _, tile = pieces[0].shape
    vmem = pl.BlockSpec(memory_space=pltpu.VMEM)
    return pl.pallas_call(
        functools.partial(place_kernel, group),
        name="place",
        out_shape=[jax.ShapeDtypeStruct((rows * group, tile), F32)] * 2,
        in_specs=[pl.BlockSpec(memory_space=pltpu.SMEM)] + [vmem] * group,
        out_specs=[vmem] * 2,
    )(at, *pieces)


def swap(x, k):
    count = lax.axis_size(GROUP)
    return lax.ppermute(x, GROUP, [(i, i ^ k) for i in range(count)])


def neighbours(x, d):
    count = lax.axis_size(BANDS)
    even = [(i, i ^ d) for i in range(count)]
    odd = [(i, ((i + d) ^ d) - d) for i in range(count)]
    odd = [(i, j) for i, j in odd if 0 <= j < count]
    return [lax.ppermute(x, BANDS, even), lax.ppermute(x, BANDS, odd)]


def stack_taps(weight, outs, channels):
    o, k = weight.shape[1:]
    w = jnp.pad(weight.reshape(3, 3, o, k), ((0, 0), (0, 0), (0, outs - o), (0, channels - k)))
    return w.transpose(0, 2, 1, 3).reshape(3 * outs, 3 * channels)


def per_device(
    left_features,
    right_features,
    left_image,
    query_key,
    value_weight,
    out_weight,
    occlusion_weight,
    first_conv,
    middle_conv,
    last_conv,
):
    height, tile, _ = left_features.shape
    group = lax.axis_size(GROUP)
    rows = height // group
    length = tile * group
    me = lax.axis_index(GROUP)
    place = lax.axis_index(BANDS)
    at = jnp.stack([me, place, jnp.int32(rows * lax.axis_size(BANDS))]).astype(jnp.int32)

    def mine(x, k, axis=0):
        return lax.dynamic_slice_in_dim(x, (me ^ k) * rows, rows, axis)

    sent = {
        k: jnp.stack([mine(left_features, k), mine(right_features, k)]) for k in range(1, group)
    }
    pieces = {k: swap(sent[k], k) for k in range(group - 1, 0, -1)}
    pieces = [pieces[k] for k in range(1, group)]

    image = left_image.astype(BF16).transpose(1, 0, 2)
    image = jnp.pad(image, ((0, 0), (2, SLOTS - 5), (0, 0)))
    strips = [mine(image, 0)] + [swap(mine(image, k), k) for k in range(1, group)]
    width = 1
    while width < group:
        high = (me & width) != 0
        strips = [
            jnp.where(
                high,
                jnp.concatenate([strips[n + 1], strips[n]], axis=2),
                jnp.concatenate([strips[n], strips[n + 1]], axis=2),
            )
            for n in range(0, len(strips), 2)
        ]
        width *= 2
    image = strips[0]

    weights = (
        query_key.T,
        query_key,
        value_weight.T,
        out_weight.T,
        occlusion_weight[:, None],
    )
    stacked, maps = attention(
        at, left_features, right_features, pieces, weights, image, rows, length
    )

    others = []
    for d in range(1, -(-RIM // rows) + 1):
        others += neighbours(stacked, d)
    first = jnp.pad(stack_taps(first_conv, CONV, SLOTS), ((0, 0), (0, SLOTS)))
    convs = (
        first,
        stack_taps(middle_conv[0], CONV, CONV),
        stack_taps(middle_conv[1], CONV, CONV),
        stack_taps(middle_conv[2], CONV, CONV),
        stack_taps(last_conv, SLOTS, CONV),
    )
    results = convolutions(at, stacked, maps, others, convs, group)
    results = [results[0]] + [swap(results[k], k) for k in range(1, group)]
    return tuple(place_rows(at, results))


def solution(mesh):
    tiles = P(("grp", "row"), ("col", "sub"))
    placed = (
        P(("grp", "row"), ("col", "sub"), None),
        P(("grp", "row"), ("col", "sub"), None),
        P(None, ("grp", "row"), ("col", "sub")),
    ) + (P(),) * 7
    return jax.shard_map(
        per_device, mesh=mesh, in_specs=placed, out_specs=(tiles, tiles), check_vma=False
    )
```

```python
import functools

import jax
import jax.numpy as jnp
from jax import lax
from jax.experimental import pallas as pl
from jax.experimental.pallas import tpu as pltpu
from jax.sharding import PartitionSpec as P

C = 128
HEADS = 8
HEAD = 16
CONV = 64
RIM = 5
SLOTS = 8
BLOCK = 128
F32 = jnp.float32
BF16 = jnp.bfloat16
GROUP = ("col", "sub")
BANDS = ("row", "col", "sub")


def dot(a, b, dims):
    return lax.dot_general(a, b, (dims, ((), ())), preferred_element_type=F32)


def attention_row(left, right, qw, kw, vw, ow, occ):
    length = left.shape[0]
    blocks = length // BLOCK
    queries = (dot(qw, left, ((1,), (1,))) * (HEAD**-0.5)).astype(BF16)
    keys = dot(right, kw, ((1,), (0,))).astype(BF16)
    values = dot(vw, right, ((1,), (1,))).astype(BF16)

    channel = lax.broadcasted_iota(jnp.int32, (1, C), 1)
    scores = []
    for j in range(blocks):
        part = keys[BLOCK * j : BLOCK * (j + 1)]
        by_head = jnp.concatenate(
            [jnp.where(channel // HEAD == h, part, jnp.zeros_like(part)) for h in range(HEADS)],
            axis=0,
        )
        scores.append(dot(by_head, queries[:, BLOCK * j :], ((1,), (0,))))

    key_at = lax.broadcasted_iota(jnp.int32, (BLOCK, BLOCK), 0)
    query_at = lax.broadcasted_iota(jnp.int32, (BLOCK, BLOCK), 1)
    allowed = key_at <= query_at
    line = lax.broadcasted_iota(jnp.int32, (HEAD, length), 0)
    place = lax.broadcasted_iota(jnp.int32, (HEAD, length), 1)
    counts = jnp.where(
        line == 0,
        1,
        jnp.where(line == 1, place % BLOCK, jnp.where(line == 2, place - place % BLOCK, 0)),
    )
    counts = counts.astype(F32).astype(BF16)

    heads = [[] for _ in range(blocks)]
    means = [jnp.zeros((1, BLOCK), F32) for _ in range(blocks)]
    for h in range(HEADS):
        stacked = jnp.concatenate([values[HEAD * h : HEAD * (h + 1)], counts], axis=0)
        for i in range(blocks):
            parts = []
            for j in range(i + 1):
                piece = scores[j][
                    BLOCK * h : BLOCK * (h + 1), BLOCK * (i - j) : BLOCK * (i - j + 1)
                ]
                if j == i:
                    piece = jnp.where(allowed, piece, -jnp.inf)
                parts.append(piece)
            largest = functools.reduce(
                jnp.maximum, [jnp.max(p, axis=0, keepdims=True) for p in parts]
            )
            expon = jnp.concatenate(
                [jnp.exp(p - largest).astype(BF16) for p in parts], axis=0
            )
            sums = dot(stacked[:, : BLOCK * (i + 1)], expon, ((1,), (0,)))
            inverse = 1.0 / sums[HEAD : HEAD + 1]
            heads[i].append((sums[:HEAD] * inverse).astype(BF16))
            means[i] = means[i] + (sums[HEAD + 1 : HEAD + 2] + sums[HEAD + 2 : HEAD + 3]) * inverse

    head_out = jnp.concatenate([jnp.concatenate(b, axis=0) for b in heads], axis=1)
    mean = jnp.concatenate(means, axis=1)
    column = lax.broadcasted_iota(jnp.int32, (1, length), 1).astype(F32)
    disparity = (HEADS * column - mean) * (8.0 / (HEADS * length))
    attended = dot(ow, head_out, ((1,), (0,)))
    centred = attended - jnp.mean(attended, axis=0, keepdims=True)
    spread = jnp.mean(centred * centred, axis=0, keepdims=True)
    occlusion = jnp.sum(centred * occ, axis=0, keepdims=True) * lax.rsqrt(spread + 1e-05)
    return disparity, occlusion


def strip_lines(rows):
    return -(-3 * rows // 16) * 16


def line_plan(cuts, tile, rows):
    sizes = [2 * c * tile + (strip_lines(rows) if n == 0 else 0) for n, c in enumerate(cuts)]
    return [(sum(sizes[:n]), s) for n, s in enumerate(sizes)]


def order(k, near):
    chip, core = k // near, k % near
    return chip * near + jnp.where(chip % 2 == 0, core, near - 1 - core)


def place_of(member, band, group, near):
    q = order(member, near)
    return jnp.where(band % 2 == 0, q, group - 1 - q)


def shared_place():
    group, near = lax.axis_size(GROUP), lax.axis_size("sub")
    me, band = lax.axis_index(GROUP), lax.axis_index("row")
    return lambda k: place_of(me ^ k, band, group, near)


def pack_kernel(partners, cuts, chunks, left, right, image, *refs):
    outs, image_s, sems, image_sem = refs[-len(partners) - 3 : -3], *refs[-3:]
    tile = image.shape[2]
    rows = sum(cuts)
    plan = line_plan(cuts, tile, rows)
    share = shared_place()
    lines = strip_lines(rows)
    copies = []
    if 0 in chunks:
        colours = pltpu.make_async_copy(image, image_s, image_sem)
        colours.start()
    n = 0
    for c in chunks:
        for k, out in zip(partners, outs):
            base = plan[c][0] - plan[chunks[0]][0]
            start = pl.multiple_of((share(k) * rows + sum(cuts[:c])) * tile, tile)
            for s, side in enumerate((left, right)):
                copy = pltpu.make_async_copy(
                    side.at[pl.ds(start, cuts[c] * tile), :],
                    out.at[pl.ds(base + s * cuts[c] * tile, cuts[c] * tile), :],
                    sems.at[n],
                )
                copy.start()
                copies.append(copy)
                n += 1
    if 0 in chunks:
        colours.wait()
        for k, out in zip(partners, outs):
            strip = [
                image_s[ch, pl.ds(pl.multiple_of(share(k) * rows, rows), rows), :]
                for ch in range(3)
            ]
            if lines > 3 * rows:
                strip.append(jnp.zeros((lines - 3 * rows, tile), F32))
            strip = jnp.concatenate(strip, axis=0)
            strip = jnp.concatenate([strip, jnp.zeros((lines, C - tile), F32)], axis=1)
            first = 2 * cuts[0] * tile
            out[first : first + lines, :] = strip.astype(BF16)
    for copy in copies:
        copy.wait()


def pack(left, right, image, partners, cuts, chunks, after=()):
    height, tile, _ = left.shape
    plan = line_plan(cuts, tile, sum(cuts))
    size = sum(plan[c][1] for c in chunks)
    vmem = pl.BlockSpec(memory_space=pltpu.VMEM)
    hbm = pl.BlockSpec(memory_space=pltpu.HBM)
    return pl.pallas_call(
        functools.partial(pack_kernel, partners, cuts, chunks),
        name="pack",
        out_shape=[jax.ShapeDtypeStruct((size, C), BF16)] * len(partners),
        in_specs=[hbm] * 3 + [vmem] * len(after),
        out_specs=[vmem] * len(partners),
        scratch_shapes=[
            pltpu.VMEM(image.shape, F32),
            pltpu.SemaphoreType.DMA((2 * len(partners) * len(chunks),)),
            pltpu.SemaphoreType.DMA,
        ],
        compiler_params=pltpu.CompilerParams(vmem_limit_bytes=16 << 20),
    )(left.reshape(height * tile, C), right.reshape(height * tile, C), image, *after)


def attention_kernel(group, near, cuts, chunk, *refs):
    pieces, (qw, kw, vw, ow, occ) = refs[:group], refs[group : group + 5]
    earlier, (stacked_ref, maps_ref, left_s, right_s) = refs[group + 5 : -4], refs[-4:]
    count, length, _ = left_s.shape
    tile = length // group
    rows, offset = sum(cuts), sum(cuts[:chunk])
    plan = line_plan(cuts, tile, rows)
    me = lax.axis_index(GROUP)
    base = [plan[chunk][0] if k < near else 0 for k in range(group)]
    for n in range(count):
        for k in range(group):
            start = pl.multiple_of((me ^ k) * tile, tile)
            line = base[k] + n * tile
            left_s[n, pl.ds(start, tile), :] = pieces[k][line : line + tile]
            line += count * tile
            right_s[n, pl.ds(start, tile), :] = pieces[k][line : line + tile]
    if chunk:
        stacked_ref[...] = earlier[0][...]
        maps_ref[...] = earlier[1][...]
    else:
        first = [b + 2 * count * tile for b in base]
        strips = [
            pieces[k][f : f + strip_lines(rows), :tile].astype(F32) for k, f in enumerate(first)
        ]
        width = 1
        while width < group:
            high = (me & width) != 0
            strips = [
                jnp.where(
                    high,
                    jnp.concatenate([strips[n + 1], strips[n]], axis=1),
                    jnp.concatenate([strips[n], strips[n + 1]], axis=1),
                )
                for n in range(0, len(strips), 2)
            ]
            width *= 2
        zero = jnp.zeros((1, length), F32)
        for r in range(rows):
            colours = [strips[0][ch * rows + r : ch * rows + r + 1] for ch in range(3)]
            stacked_ref[r] = jnp.concatenate(
                [zero, zero] + colours + [zero] * (SLOTS - 5), axis=0
            ).astype(BF16)
    slot = lax.broadcasted_iota(jnp.int32, (SLOTS, 1), 0)
    for n in range(count):
        r = offset + n
        disparity, occlusion = attention_row(
            left_s[n], right_s[n], qw[...], kw[...], vw[...], ow[...], occ[...]
        )
        maps_ref[r] = jnp.concatenate([disparity, occlusion], axis=0)
        full = jnp.where(slot == 0, disparity, stacked_ref[r].astype(F32))
        stacked_ref[r] = jnp.where(slot == 1, occlusion, full).astype(BF16)


def attention(pieces, weights, earlier, near, cuts, length):
    group = len(pieces)
    chunk = 0 if not earlier else earlier[2]
    rows, count = sum(cuts), cuts[chunk]
    vmem = pl.BlockSpec(memory_space=pltpu.VMEM)
    pairs = count * HEADS * length * length
    results = pl.pallas_call(
        functools.partial(attention_kernel, group, near, cuts, chunk),
        name="attention",
        out_shape=(
            jax.ShapeDtypeStruct((rows, SLOTS, length), BF16),
            jax.ShapeDtypeStruct((rows, 2, length), F32),
        ),
        in_specs=[vmem] * (group + len(weights) + len(earlier[:2])),
        out_specs=(vmem, vmem),
        scratch_shapes=[pltpu.VMEM((count, length, C), BF16)] * 2,
        compiler_params=pltpu.CompilerParams(vmem_limit_bytes=24 << 20),
        cost_estimate=pl.CostEstimate(
            flops=pairs * 4 * C, transcendentals=pairs, bytes_accessed=8 * count * length * C
        ),
    )(*pieces, *weights, *earlier[:2])
    return (*results, chunk + 1)


def spread_taps(x):
    length = x.shape[1]
    column = lax.broadcasted_iota(jnp.int32, (1, length), 1)
    before = jnp.where(column == 0, 0.0, pltpu.roll(x, 1, 1))
    after = jnp.where(column == length - 1, 0.0, pltpu.roll(x, length - 1, 1))
    return before, x, after


def conv_rows(source, weight, outs, count, finish):
    def at(q):
        p = dot(weight[...], source[q], ((1,), (0,)))
        return p[:outs], p[outs : 2 * outs], p[2 * outs :]

    top0, top1, _ = at(0)
    next0, next1, _ = at(1)
    del top1

    def body(r, carry):
        first, second = carry
        p0, p1, p2 = at(r + 2)
        finish(r, first + p2)
        return second + p1, p0

    carry = (top0 + next1, next0)
    for r in range(count):
        carry = body(r, carry)


def conv_kernel(group, hops, own, maps, *refs):
    others = refs[: 2 * hops]
    w1, w2, w3, w4, w5 = refs[2 * hops : 2 * hops + 5]
    outs = refs[2 * hops + 5 : 2 * hops + 5 + group]
    x0, x1, x2, x3, x4 = refs[2 * hops + 5 + group :]
    rows, _, length = own.shape
    me = lax.axis_index(GROUP)
    place = lax.axis_index("row") * group + shared_place()(0)
    last = lax.axis_size(BANDS) * rows
    base = place * rows

    def put(q, block):
        before, same, after = spread_taps(block.astype(F32))
        zero = jnp.zeros_like(same)
        x0[q] = jnp.concatenate([before, same, after, zero], axis=0).astype(BF16)

    for q in range(rows):
        put(RIM + q, own[q])
    for d in range(1, hops + 1):
        flag = jnp.bitwise_and(place, d) != 0
        a, b = others[2 * d - 2], others[2 * d - 1]
        for q in range(rows):
            up = RIM - d * rows + q
            if up >= 0:
                put(up, jnp.where(flag, a[q], b[q]))
            down = RIM + d * rows + q
            if down < rows + 2 * RIM:
                put(down, jnp.where(flag, b[q], a[q]))

    def store(target, lead, residual=None):
        def finish(r, total):
            if residual is not None:
                total = total + residual[r + 2, CONV : 2 * CONV].astype(F32)
            g = base + r - lead
            inside = jnp.logical_and(g >= 0, g < last)
            y = jnp.where(inside, jnp.maximum(total, 0.0), 0.0)
            before, same, after = spread_taps(y)
            target[r, :CONV] = before.astype(BF16)
            target[r, CONV : 2 * CONV] = same.astype(BF16)
            target[r, 2 * CONV :] = after.astype(BF16)

        return finish

    conv_rows(x0, w1, CONV, rows + 8, store(x1, 4))
    conv_rows(x1, w2, CONV, rows + 6, store(x2, 3))
    conv_rows(x2, w3, CONV, rows + 4, store(x3, 2, x1))
    conv_rows(x3, w4, CONV, rows + 2, store(x4, 1))

    tile = length // group

    def last_row(r, total):
        m = maps[r]
        disparity = m[:1] + total[:1]
        occlusion = jax.nn.sigmoid(m[1:2] + total[1:2])
        finals[0].append(disparity)
        finals[1].append(occlusion)

    finals = [], []
    conv_rows(x4, w5, SLOTS, rows, last_row)
    for n in range(2):
        both = jnp.concatenate(finals[n], axis=0)
        cut = [both[:, tile * c : tile * (c + 1)] for c in range(group)]
        for k in range(group):
            pick = cut[0]
            for c in range(1, group):
                pick = jnp.where((me ^ k) == c, cut[c], pick)
            outs[k][n] = pick


def convolutions(own, maps, others, weights, group):
    rows, _, length = own.shape
    tile = length // group
    hops = len(others) // 2
    vmem = pl.BlockSpec(memory_space=pltpu.VMEM)
    depth = 3 * CONV
    return pl.pallas_call(
        functools.partial(conv_kernel, group, hops),
        name="convolutions",
        out_shape=[jax.ShapeDtypeStruct((2, rows, tile), F32)] * group,
        in_specs=[vmem] * (2 + len(others) + len(weights)),
        out_specs=[vmem] * group,
        scratch_shapes=[
            pltpu.VMEM((rows + 10, 4 * SLOTS, length), BF16),
            pltpu.VMEM((rows + 8, depth, length), BF16),
            pltpu.VMEM((rows + 6, depth, length), BF16),
            pltpu.VMEM((rows + 4, depth, length), BF16),
            pltpu.VMEM((rows + 2, depth, length), BF16),
        ],
        compiler_params=pltpu.CompilerParams(vmem_limit_bytes=40 << 20),
    )(own, maps, *others, *weights)


def place_kernel(group, *refs):
    pieces, outs = refs[:group], refs[group:]
    rows = pieces[0].shape[1]
    share = shared_place()
    for k in range(group):
        start = pl.multiple_of(share(k) * rows, rows)
        for n in range(2):
            outs[n][pl.ds(start, rows), :] = pieces[k][n]


def place_rows(pieces):
    group = len(pieces)
    _, rows, tile = pieces[0].shape
    vmem = pl.BlockSpec(memory_space=pltpu.VMEM)
    return pl.pallas_call(
        functools.partial(place_kernel, group),
        name="place",
        out_shape=[jax.ShapeDtypeStruct((rows * group, tile), F32)] * 2,
        in_specs=[vmem] * group,
        out_specs=[vmem] * 2,
        compiler_params=pltpu.CompilerParams(vmem_limit_bytes=4 << 20),
    )(*pieces)


def swap(x, k):
    count = lax.axis_size(GROUP)
    return lax.ppermute(x, GROUP, [(i, i ^ k) for i in range(count)])


def neighbours(x, d):
    count, group, near = lax.axis_size(BANDS), lax.axis_size(GROUP), lax.axis_size("sub")

    def device(place):
        band, q = divmod(place, group)
        chip, core = divmod(q if band % 2 == 0 else group - 1 - q, near)
        return band * group + chip * near + (core if chip % 2 == 0 else near - 1 - core)

    even = [(i, i ^ d) for i in range(count)]
    odd = [(i, ((i + d) ^ d) - d) for i in range(count)]
    return [
        lax.ppermute(x, BANDS, [(device(i), device(j)) for i, j in pairs if 0 <= j < count])
        for pairs in (even, odd)
    ]


def chunks_of(rows):
    first = -(-5 * rows // 8)
    return (first, rows - first)


def stack_taps(weight, outs, channels):
    o, k = weight.shape[1:]
    w = jnp.pad(weight.reshape(3, 3, o, k), ((0, 0), (0, 0), (0, outs - o), (0, channels - k)))
    return w.transpose(0, 2, 1, 3).reshape(3 * outs, 3 * channels)


def per_device(
    left_features,
    right_features,
    left_image,
    query_key,
    value_weight,
    out_weight,
    occlusion_weight,
    first_conv,
    middle_conv,
    last_conv,
):
    height, tile, _ = left_features.shape
    group = lax.axis_size(GROUP)
    rows = height // group
    length = tile * group
    near = lax.axis_size("sub")
    cuts = chunks_of(rows)
    features = (left_features, right_features, left_image)
    chunks = tuple(range(len(cuts)))
    distant = tuple(range(near, group))
    close = pack(*features, tuple(range(near)), cuts, chunks)
    packed = pack(*features, distant, cuts, (0,))
    tables = (first_conv, middle_conv, last_conv, query_key, value_weight, out_weight)
    close, packed, tables = lax.optimization_barrier((close, packed, tables))
    first_conv, middle_conv, last_conv, query_key, value_weight, out_weight = tables
    far = [[swap(x, k) for k, x in zip(distant, packed)][::1]]
    close = [close[0]] + [swap(close[k], k) for k in range(1, near)]
    for c in chunks[1:]:
        packed = pack(*features, distant, cuts, (c,), (close[-1],))
        far.append([swap(x, k) for k, x in zip(distant, packed)])

    weights = (
        query_key.T,
        query_key,
        value_weight.T,
        out_weight.T,
        occlusion_weight[:, None],
    )
    first = jnp.pad(stack_taps(first_conv, CONV, SLOTS), ((0, 0), (0, SLOTS)))
    convs = (
        first,
        stack_taps(middle_conv[0], CONV, CONV),
        stack_taps(middle_conv[1], CONV, CONV),
        stack_taps(middle_conv[2], CONV, CONV),
        stack_taps(last_conv, SLOTS, CONV),
    )
    weights, convs = lax.optimization_barrier((weights, convs))
    done = ()
    for c in range(len(cuts)):
        done = attention(close + far[c], weights, done, near, cuts, length)
    stacked, maps, _ = done

    others = []
    for d in range(1, -(-RIM // rows) + 1):
        others += neighbours(stacked, d)
    results = convolutions(stacked, maps, others, convs, group)
    results = [results[0]] + [swap(results[k], k) for k in range(1, group)]
    return tuple(place_rows(results))


def solution(mesh):
    tiles = P(("grp", "row"), ("col", "sub"))
    placed = (
        P(("grp", "row"), ("col", "sub"), None),
        P(("grp", "row"), ("col", "sub"), None),
        P(None, ("grp", "row"), ("col", "sub")),
    ) + (P(),) * 7
    return jax.shard_map(
        per_device, mesh=mesh, in_specs=placed, out_specs=(tiles, tiles), check_vma=False
    )
```

```python
import functools

import jax
import jax.numpy as jnp
from jax import lax
from jax.experimental import pallas as pl
from jax.experimental.pallas import tpu as pltpu
from jax.sharding import PartitionSpec as P

C = 128
HEADS = 8
HEAD = 16
CONV = 64
RIM = 5
SLOTS = 8
BLOCK = 128
F32 = jnp.float32
BF16 = jnp.bfloat16
GROUP = ("col", "sub")
BANDS = ("row", "col", "sub")


def dot(a, b, dims):
    return lax.dot_general(a, b, (dims, ((), ())), preferred_element_type=F32)


def score_blocks(queries, keys):
    channel = lax.broadcasted_iota(jnp.int32, (1, C), 1)
    found = []
    for j in range(keys.shape[0] // BLOCK):
        part = keys[BLOCK * j : BLOCK * (j + 1)]
        by_head = [
            jnp.where(channel // HEAD == h, part, jnp.zeros_like(part)) for h in range(HEADS)
        ]
        s = dot(jnp.concatenate(by_head, axis=0), queries[:, BLOCK * j :], ((1,), (0,)))
        found.append([s[:, i : i + BLOCK] for i in range(0, s.shape[1], BLOCK)])
    return found


def attention_row(left, right, qw, kw, vw, ow, occ):
    length = left.shape[0]
    blocks = length // BLOCK
    queries = (dot(qw, left, ((1,), (1,))) * (HEAD**-0.5)).astype(BF16)
    keys = dot(right, kw, ((1,), (0,))).astype(BF16)
    values = dot(vw, right, ((1,), (1,))).astype(BF16)
    scores = score_blocks(queries, keys)

    key_at = lax.broadcasted_iota(jnp.int32, (BLOCK, BLOCK), 0)
    query_at = lax.broadcasted_iota(jnp.int32, (BLOCK, BLOCK), 1)
    allowed = key_at <= query_at
    line = lax.broadcasted_iota(jnp.int32, (HEAD, length), 0)
    place = lax.broadcasted_iota(jnp.int32, (HEAD, length), 1)
    counts = jnp.where(
        line == 0,
        1,
        jnp.where(line == 1, place % BLOCK, jnp.where(line == 2, place - place % BLOCK, 0)),
    )
    counts = counts.astype(F32).astype(BF16)

    heads = [[] for _ in range(blocks)]
    means = [jnp.zeros((1, BLOCK), F32) for _ in range(blocks)]
    for h in range(0, HEADS, 2):
        stacked = jnp.concatenate([values[HEAD * h : HEAD * (h + 2)], counts], axis=0)
        for i in range(blocks):
            expon = []
            for g in (h, h + 1):
                parts = [scores[j][i - j][BLOCK * g : BLOCK * (g + 1)] for j in range(i + 1)]
                parts[i] = jnp.where(allowed, parts[i], -jnp.inf)
                largest = functools.reduce(
                    jnp.maximum, [jnp.max(p, axis=0, keepdims=True) for p in parts]
                )
                expon.append(
                    jnp.concatenate([jnp.exp(p - largest).astype(BF16) for p in parts], axis=0)
                )
            sums = dot(
                stacked[:, : BLOCK * (i + 1)], jnp.concatenate(expon, axis=1), ((1,), (0,))
            )
            for g in range(2):
                part = sums[:, BLOCK * g : BLOCK * (g + 1)]
                inverse = 1.0 / part[2 * HEAD : 2 * HEAD + 1]
                heads[i].append((part[HEAD * g : HEAD * (g + 1)] * inverse).astype(BF16))
                total = part[2 * HEAD + 1 : 2 * HEAD + 2] + part[2 * HEAD + 2 : 2 * HEAD + 3]
                means[i] = means[i] + total * inverse

    head_out = jnp.concatenate([jnp.concatenate(b, axis=0) for b in heads], axis=1)
    mean = jnp.concatenate(means, axis=1)
    column = lax.broadcasted_iota(jnp.int32, (1, length), 1).astype(F32)
    disparity = (HEADS * column - mean) * (8.0 / (HEADS * length))
    attended = dot(ow, head_out, ((1,), (0,)))
    centred = attended - jnp.mean(attended, axis=0, keepdims=True)
    spread = jnp.mean(centred * centred, axis=0, keepdims=True)
    occlusion = jnp.sum(centred * occ, axis=0, keepdims=True) * lax.rsqrt(spread + 1e-05)
    return disparity, occlusion


def strip_lines(rows):
    return -(-3 * rows // 16) * 16


def order(k, near):
    chip, core = k // near, k % near
    return chip * near + jnp.where(chip % 2 == 0, core, near - 1 - core)


def place_of(member, band, group, near):
    q = order(member, near)
    return jnp.where(band % 2 == 0, q, group - 1 - q)


def shared_place():
    group, near = lax.axis_size(GROUP), lax.axis_size("sub")
    me, band = lax.axis_index(GROUP), lax.axis_index("row")
    return lambda k: place_of(me ^ k, band, group, near)


def chunk_start(place, cuts, chunk):
    start = sum(cuts[:chunk])
    return jnp.where(place % 2 == 0, start, sum(cuts) - start - cuts[chunk])


def pack_kernel(chunk, cuts, left, right, image, *refs):
    group = lax.axis_size(GROUP)
    outs, image_s, sems, image_sem = refs[-group - 3 : -3], *refs[-3:]
    tile = image.shape[2]
    rows, lines = sum(cuts), cuts[chunk] * tile
    share = shared_place()
    copies = []

    def send(source, target):
        copy = pltpu.make_async_copy(source, target, sems.at[len(copies)])
        copy.start()
        copies.append(copy)

    if chunk == 0:
        colours = pltpu.make_async_copy(image, image_s, image_sem)
        colours.start()
    for k in range(group):
        first = share(k) * rows + chunk_start(share(k), cuts, chunk)
        first = pl.multiple_of(first * tile, tile)
        for s, side in enumerate((left, right)):
            send(side.at[pl.ds(first, lines), :], outs[k].at[pl.ds(s * lines, lines), :])
    if chunk == 0:
        count = strip_lines(rows)
        colours.wait()
        for k in range(group):
            start = pl.multiple_of(share(k) * rows, rows)
            strip = [image_s[ch, pl.ds(start, rows), :] for ch in range(3)]
            if count > 3 * rows:
                strip.append(jnp.zeros((count - 3 * rows, tile), F32))
            strip = jnp.concatenate(strip, axis=0)
            strip = jnp.concatenate([strip, jnp.zeros((count, C - tile), F32)], axis=1)
            outs[k][2 * lines : 2 * lines + count, :] = strip.astype(BF16)
    for copy in copies:
        copy.wait()


def pack(left, right, image, chunk, cuts, after=()):
    height, tile, _ = left.shape
    group = lax.axis_size(GROUP)
    count = strip_lines(sum(cuts))
    size = 2 * cuts[chunk] * tile + (count if chunk == 0 else 0)
    vmem = pl.BlockSpec(memory_space=pltpu.VMEM)
    hbm = pl.BlockSpec(memory_space=pltpu.HBM)
    return pl.pallas_call(
        functools.partial(pack_kernel, chunk, cuts),
        name="pack",
        out_shape=[jax.ShapeDtypeStruct((size, C), BF16)] * group,
        in_specs=[hbm] * 3 + [vmem] * len(after),
        out_specs=[vmem] * group,
        scratch_shapes=[
            pltpu.VMEM(image.shape, F32),
            pltpu.SemaphoreType.DMA((2 * group,)),
            pltpu.SemaphoreType.DMA,
        ],
        compiler_params=pltpu.CompilerParams(vmem_limit_bytes=(16 if after else 60) << 20),
    )(left.reshape(height * tile, C), right.reshape(height * tile, C), image, *after)


def weight_kernel(qk, value, out, occ, first, middle, last, *outs):
    q_t, v_t, o_t, occ_t, w1, w2, w3, w4, w5 = outs

    def flip(x):
        return jnp.transpose(x.astype(F32)).astype(BF16)

    q_t[...], v_t[...], o_t[...] = flip(qk[...]), flip(value[...]), flip(out[...])
    occ_t[...] = jnp.transpose(jnp.broadcast_to(occ[...], (C, C)))[:, :1]
    for a in range(3):
        block = []
        for b in range(3):
            block.append(first[3 * a + b].astype(F32))
            block.append(jnp.zeros((SLOTS - first.shape[1], CONV), F32))
        block.append(jnp.zeros((C - 3 * SLOTS, CONV), F32))
        block = jnp.concatenate(block, axis=0)
        block = jnp.concatenate([block, jnp.zeros((C, C - CONV), F32)], axis=1)
        w1[CONV * a : CONV * (a + 1), :] = jnp.transpose(block)[:CONV, : 4 * SLOTS].astype(BF16)
        for n, w in enumerate((w2, w3, w4)):
            taps = [middle[9 * n + 3 * a + b] for b in range(3)]
            w[CONV * a : CONV * (a + 1), :] = jnp.concatenate(taps, axis=1)
        taps = jnp.concatenate([last[3 * a + b].astype(F32) for b in range(3)], axis=1)
        taps = jnp.concatenate([taps, jnp.zeros((SLOTS - 2, 3 * CONV), F32)], axis=0)
        rest = taps if a == 0 else jnp.concatenate([rest, taps], axis=0)
    w5[...] = rest.astype(BF16)


def prepare_weights(qk, value, out, occ, first, middle, last):
    vmem = pl.BlockSpec(memory_space=pltpu.VMEM)
    square = jax.ShapeDtypeStruct((C, C), BF16)
    deep = jax.ShapeDtypeStruct((3 * CONV, 3 * CONV), BF16)
    results = pl.pallas_call(
        weight_kernel,
        name="weights",
        out_shape=[
            square,
            square,
            square,
            jax.ShapeDtypeStruct((C, 1), F32),
            jax.ShapeDtypeStruct((3 * CONV, 4 * SLOTS), BF16),
            deep,
            deep,
            deep,
            jax.ShapeDtypeStruct((3 * SLOTS, 3 * CONV), BF16),
        ],
        in_specs=[vmem] * 7,
        out_specs=[vmem] * 9,
        compiler_params=pltpu.CompilerParams(vmem_limit_bytes=16 << 20),
    )(
        qk,
        value,
        out,
        occ[None],
        first.transpose(0, 2, 1),
        middle.reshape(27, CONV, CONV),
        last,
    )
    q_t, v_t, o_t, occ_t, *convs = results
    return (q_t, qk, v_t, o_t, occ_t), tuple(convs)


def attention_kernel(cuts, chunk, *refs):
    group = lax.axis_size(GROUP)
    pieces, (qw, kw, vw, ow, occ) = refs[:group], refs[group : group + 5]
    earlier, (stacked_ref, maps_ref, left_s, right_s) = refs[group + 5 : -4], refs[-4:]
    count, length, _ = left_s.shape
    tile = length // group
    rows = sum(cuts)
    me, place = lax.axis_index(GROUP), shared_place()(0)
    for n in range(count):
        for k in range(group):
            start = pl.multiple_of((me ^ k) * tile, tile)
            left_s[n, pl.ds(start, tile), :] = pieces[k][n * tile : (n + 1) * tile]
            line = (count + n) * tile
            right_s[n, pl.ds(start, tile), :] = pieces[k][line : line + tile]
    slot = lax.broadcasted_iota(jnp.int32, (SLOTS, 1), 0)
    if chunk:
        stacked_ref[...] = earlier[0][...]
        maps_ref[...] = earlier[1][...]
    else:
        line = 2 * count * tile
        strips = [p[line : line + strip_lines(rows), :tile].astype(F32) for p in pieces]
        width = 1
        while width < group:
            high = (me & width) != 0
            strips = [
                jnp.where(
                    high,
                    jnp.concatenate([strips[n + 1], strips[n]], axis=1),
                    jnp.concatenate([strips[n], strips[n + 1]], axis=1),
                )
                for n in range(0, len(strips), 2)
            ]
            width *= 2
        zero = jnp.zeros((1, length), F32)
        for r in range(rows):
            colours = [strips[0][ch * rows + r : ch * rows + r + 1] for ch in range(3)]
            stacked_ref[r] = jnp.concatenate(
                [zero, zero] + colours + [zero] * (SLOTS - 5), axis=0
            ).astype(BF16)
        maps_ref[...] = jnp.zeros_like(maps_ref)
    first = chunk_start(place, cuts, chunk)
    for n in range(count):
        disparity, occlusion = attention_row(
            left_s[n], right_s[n], qw[...], kw[...], vw[...], ow[...], occ[...]
        )
        r = first + n
        maps_ref[r] = jnp.concatenate([disparity, occlusion], axis=0)
        full = jnp.where(slot == 0, disparity, stacked_ref[r].astype(F32))
        stacked_ref[r] = jnp.where(slot == 1, occlusion, full).astype(BF16)


def attention(pieces, weights, earlier, cuts, chunk, length):
    rows, count = sum(cuts), cuts[chunk]
    vmem = pl.BlockSpec(memory_space=pltpu.VMEM)
    pairs = count * HEADS * length * length
    return pl.pallas_call(
        functools.partial(attention_kernel, cuts, chunk),
        name="attention",
        out_shape=(
            jax.ShapeDtypeStruct((rows, SLOTS, length), BF16),
            jax.ShapeDtypeStruct((rows, 2, length), F32),
        ),
        in_specs=[vmem] * (len(pieces) + len(weights) + len(earlier)),
        out_specs=(vmem, vmem),
        scratch_shapes=[pltpu.VMEM((count, length, C), BF16)] * 2,
        compiler_params=pltpu.CompilerParams(vmem_limit_bytes=24 << 20),
        cost_estimate=pl.CostEstimate(
            flops=pairs * 4 * C, transcendentals=pairs, bytes_accessed=8 * count * length * C
        ),
    )(*pieces, *weights, *earlier)


def spread_taps(x):
    length = x.shape[1]
    column = lax.broadcasted_iota(jnp.int32, (1, length), 1)
    before = jnp.where(column == 0, 0.0, pltpu.roll(x, 1, 1))
    after = jnp.where(column == length - 1, 0.0, pltpu.roll(x, length - 1, 1))
    return before, x, after


def conv_rows(source, weight, outs, count, finish):
    def at(q):
        p = dot(weight[...], source[q], ((1,), (0,)))
        return p[:outs], p[outs : 2 * outs], p[2 * outs :]

    top0, top1, _ = at(0)
    next0, next1, _ = at(1)
    del top1

    def body(r, carry):
        first, second = carry
        p0, p1, p2 = at(r + 2)
        finish(r, first + p2)
        return second + p1, p0

    carry = (top0 + next1, next0)
    for r in range(count):
        carry = body(r, carry)


def conv_kernel(group, hops, own, maps, *refs):
    others = refs[: 2 * hops]
    w1, w2, w3, w4, w5 = refs[2 * hops : 2 * hops + 5]
    outs = refs[2 * hops + 5 : 2 * hops + 5 + group]
    x0, x1, x2, x3, x4 = refs[2 * hops + 5 + group :]
    rows, _, length = own.shape
    me = lax.axis_index(GROUP)
    place = lax.axis_index("row") * group + shared_place()(0)
    last = lax.axis_size(BANDS) * rows
    base = place * rows

    def put(q, block):
        before, same, after = spread_taps(block.astype(F32))
        zero = jnp.zeros_like(same)
        x0[q] = jnp.concatenate([before, same, after, zero], axis=0).astype(BF16)

    for q in range(rows):
        put(RIM + q, own[q])
    for d in range(1, hops + 1):
        flag = jnp.bitwise_and(place, d) != 0
        a, b = others[2 * d - 2], others[2 * d - 1]
        for q in range(rows):
            up = RIM - d * rows + q
            if up >= 0:
                inside = base - d * rows >= 0
                put(up, jnp.where(inside, jnp.where(flag, a[q], b[q]).astype(F32), 0.0))
            down = RIM + d * rows + q
            if down < rows + 2 * RIM:
                inside = base + d * rows < last
                put(down, jnp.where(inside, jnp.where(flag, b[q], a[q]).astype(F32), 0.0))

    def store(target, lead, residual=None):
        def finish(r, total):
            if residual is not None:
                total = total + residual[r + 2, CONV : 2 * CONV].astype(F32)
            g = base + r - lead
            inside = jnp.logical_and(g >= 0, g < last)
            y = jnp.where(inside, jnp.maximum(total, 0.0), 0.0)
            before, same, after = spread_taps(y)
            target[r, :CONV] = before.astype(BF16)
            target[r, CONV : 2 * CONV] = same.astype(BF16)
            target[r, 2 * CONV :] = after.astype(BF16)

        return finish

    conv_rows(x0, w1, CONV, rows + 8, store(x1, 4))
    conv_rows(x1, w2, CONV, rows + 6, store(x2, 3))
    conv_rows(x2, w3, CONV, rows + 4, store(x3, 2, x1))
    conv_rows(x3, w4, CONV, rows + 2, store(x4, 1))

    tile = length // group

    def last_row(r, total):
        m = maps[r]
        disparity = m[:1] + total[:1]
        occlusion = jax.nn.sigmoid(m[1:2] + total[1:2])
        finals[0].append(disparity)
        finals[1].append(occlusion)

    finals = [], []
    conv_rows(x4, w5, SLOTS, rows, last_row)
    for n in range(2):
        both = jnp.concatenate(finals[n], axis=0)
        cut = [both[:, tile * c : tile * (c + 1)] for c in range(group)]
        for k in range(group):
            pick = cut[0]
            for c in range(1, group):
                pick = jnp.where((me ^ k) == c, cut[c], pick)
            outs[k][n] = pick


def convolutions(own, maps, others, weights, group):
    rows, _, length = own.shape
    tile = length // group
    hops = len(others) // 2
    vmem = pl.BlockSpec(memory_space=pltpu.VMEM)
    depth = 3 * CONV
    return pl.pallas_call(
        functools.partial(conv_kernel, group, hops),
        name="convolutions",
        out_shape=[jax.ShapeDtypeStruct((2, rows, tile), F32)] * group,
        in_specs=[vmem] * (2 + len(others) + len(weights)),
        out_specs=[vmem] * group,
        scratch_shapes=[
            pltpu.VMEM((rows + 10, 4 * SLOTS, length), BF16),
            pltpu.VMEM((rows + 8, depth, length), BF16),
            pltpu.VMEM((rows + 6, depth, length), BF16),
            pltpu.VMEM((rows + 4, depth, length), BF16),
            pltpu.VMEM((rows + 2, depth, length), BF16),
        ],
        compiler_params=pltpu.CompilerParams(vmem_limit_bytes=40 << 20),
    )(own, maps, *others, *weights)


def place_kernel(group, *refs):
    pieces, outs = refs[:group], refs[group:]
    rows = pieces[0].shape[1]
    share = shared_place()
    for k in range(group):
        start = pl.multiple_of(share(k) * rows, rows)
        for n in range(2):
            outs[n][pl.ds(start, rows), :] = pieces[k][n]


def place_rows(pieces):
    group = len(pieces)
    _, rows, tile = pieces[0].shape
    vmem = pl.BlockSpec(memory_space=pltpu.VMEM)
    return pl.pallas_call(
        functools.partial(place_kernel, group),
        name="place",
        out_shape=[jax.ShapeDtypeStruct((rows * group, tile), F32)] * 2,
        in_specs=[vmem] * group,
        out_specs=[vmem] * 2,
        compiler_params=pltpu.CompilerParams(vmem_limit_bytes=4 << 20),
    )(*pieces)


def swap(x, k):
    count = lax.axis_size(GROUP)
    return lax.ppermute(x, GROUP, [(i, i ^ k) for i in range(count)])


def neighbours(x, d, odd):
    count, group, near = lax.axis_size(BANDS), lax.axis_size(GROUP), lax.axis_size("sub")

    def device(place):
        band, q = divmod(place, group)
        chip, core = divmod(q if band % 2 == 0 else group - 1 - q, near)
        return band * group + chip * near + (core if chip % 2 == 0 else near - 1 - core)

    pairs = [(i, ((i + d) ^ d) - d if odd else i ^ d) for i in range(count)]
    parts = lax.axis_size("grp")
    targets = []
    for part in range(parts):
        for i, j in pairs:
            at = part
            if not 0 <= j < count:
                at, j = (part ^ 1 if part ^ 1 < parts else part), i
            targets.append((part * count + device(i), at * count + device(j)))
    return lax.ppermute(x, ("grp",) + BANDS, targets)


def chunks_of(rows):
    first = -(-5 * rows // 8)
    return (first, rows - first)


def per_device(
    left_features,
    right_features,
    left_image,
    query_key,
    value_weight,
    out_weight,
    occlusion_weight,
    first_conv,
    middle_conv,
    last_conv,
):
    height, tile, _ = left_features.shape
    group = lax.axis_size(GROUP)
    rows = height // group
    length = tile * group
    cuts = chunks_of(rows)
    features = (left_features, right_features, left_image)
    packed = pack(*features, 0, cuts)
    tables = (
        query_key,
        value_weight,
        out_weight,
        occlusion_weight,
        first_conv,
        middle_conv,
        last_conv,
    )
    packed, tables = lax.optimization_barrier((packed, tables))
    pieces = []
    for c in range(len(cuts)):
        if c:
            packed = pack(*features, c, cuts, (pieces[-1][1],))
        pieces.append([packed[0]] + [swap(packed[k], k) for k in range(1, group)])

    weights, convs = prepare_weights(*tables)
    weights, convs = lax.optimization_barrier((weights, convs))
    done = ()
    others = []
    hops = -(-RIM // rows)
    for c in range(len(cuts)):
        done = attention(pieces[c], weights, done, cuts, c, length)
        if hops == 1 and len(others) == 0 and sum(cuts[: c + 1]) >= RIM:
            others = [neighbours(done[0], 1, True)]
    stacked, maps = done
    if hops == 1:
        others = [neighbours(stacked, 1, False)] + others
    else:
        for d in range(1, hops + 1):
            others += [neighbours(stacked, d, odd) for odd in (False, True)]
    results = convolutions(stacked, maps, others, convs, group)
    results = [results[0]] + [swap(results[k], k) for k in range(1, group)]
    return tuple(place_rows(results))


def solution(mesh):
    tiles = P(("grp", "row"), ("col", "sub"))
    placed = (
        P(("grp", "row"), ("col", "sub"), None),
        P(("grp", "row"), ("col", "sub"), None),
        P(None, ("grp", "row"), ("col", "sub")),
    ) + (P(),) * 7
    return jax.shard_map(
        per_device, mesh=mesh, in_specs=placed, out_specs=(tiles, tiles), check_vma=False
    )
```

```python
import functools

import jax
import jax.numpy as jnp
from jax import lax
from jax.experimental import pallas as pl
from jax.experimental.pallas import tpu as pltpu
from jax.sharding import PartitionSpec as P

C = 128
HEADS = 8
HEAD = 16
CONV = 64
RIM = 5
SLOTS = 8
BLOCK = 128
F32 = jnp.float32
BF16 = jnp.bfloat16
GROUP = ("col", "sub")
BANDS = ("row", "col", "sub")


def dot(a, b, dims):
    return lax.dot_general(a, b, (dims, ((), ())), preferred_element_type=F32)


def score_blocks(queries, keys):
    channel = lax.broadcasted_iota(jnp.int32, (1, C), 1)
    found = []
    for j in range(keys.shape[0] // BLOCK):
        part = keys[BLOCK * j : BLOCK * (j + 1)]
        by_head = [
            jnp.where(channel // HEAD == h, part, jnp.zeros_like(part)) for h in range(HEADS)
        ]
        s = dot(jnp.concatenate(by_head, axis=0), queries[:, BLOCK * j :], ((1,), (0,)))
        found.append([s[:, i : i + BLOCK] for i in range(0, s.shape[1], BLOCK)])
    return found


def attention_row(left, right, qw, kw, vw, ow, occ):
    length = left.shape[0]
    blocks = length // BLOCK
    queries = (dot(qw, left, ((1,), (1,))) * (HEAD**-0.5)).astype(BF16)
    keys = dot(right, kw, ((1,), (0,))).astype(BF16)
    values = dot(vw, right, ((1,), (1,))).astype(BF16)
    scores = score_blocks(queries, keys)

    key_at = lax.broadcasted_iota(jnp.int32, (BLOCK, BLOCK), 0)
    query_at = lax.broadcasted_iota(jnp.int32, (BLOCK, BLOCK), 1)
    allowed = key_at <= query_at
    line = lax.broadcasted_iota(jnp.int32, (HEAD, length), 0)
    place = lax.broadcasted_iota(jnp.int32, (HEAD, length), 1)
    counts = jnp.where(
        line == 0,
        1,
        jnp.where(line == 1, place % BLOCK, jnp.where(line == 2, place - place % BLOCK, 0)),
    )
    counts = counts.astype(F32).astype(BF16)

    heads = [[] for _ in range(blocks)]
    means = [jnp.zeros((1, BLOCK), F32) for _ in range(blocks)]
    for h in range(0, HEADS, 2):
        stacked = jnp.concatenate([values[HEAD * h : HEAD * (h + 2)], counts], axis=0)
        for i in range(blocks):
            expon = []
            for g in (h, h + 1):
                parts = [scores[j][i - j][BLOCK * g : BLOCK * (g + 1)] for j in range(i + 1)]
                parts[i] = jnp.where(allowed, parts[i], -jnp.inf)
                largest = functools.reduce(
                    jnp.maximum, [jnp.max(p, axis=0, keepdims=True) for p in parts]
                )
                expon.append(
                    jnp.concatenate([jnp.exp(p - largest).astype(BF16) for p in parts], axis=0)
                )
            sums = dot(
                stacked[:, : BLOCK * (i + 1)], jnp.concatenate(expon, axis=1), ((1,), (0,))
            )
            for g in range(2):
                part = sums[:, BLOCK * g : BLOCK * (g + 1)]
                inverse = 1.0 / part[2 * HEAD : 2 * HEAD + 1]
                heads[i].append((part[HEAD * g : HEAD * (g + 1)] * inverse).astype(BF16))
                total = part[2 * HEAD + 1 : 2 * HEAD + 2] + part[2 * HEAD + 2 : 2 * HEAD + 3]
                means[i] = means[i] + total * inverse

    head_out = jnp.concatenate([jnp.concatenate(b, axis=0) for b in heads], axis=1)
    mean = jnp.concatenate(means, axis=1)
    column = lax.broadcasted_iota(jnp.int32, (1, length), 1).astype(F32)
    disparity = (HEADS * column - mean) * (8.0 / (HEADS * length))
    attended = dot(ow, head_out, ((1,), (0,)))
    centred = attended - jnp.mean(attended, axis=0, keepdims=True)
    spread = jnp.mean(centred * centred, axis=0, keepdims=True)
    occlusion = jnp.sum(centred * occ, axis=0, keepdims=True) * lax.rsqrt(spread + 1e-05)
    return disparity, occlusion


def strip_lines(rows):
    return -(-3 * rows // 16) * 16


def order(k, near):
    chip, core = k // near, k % near
    return chip * near + jnp.where(chip % 2 == 0, core, near - 1 - core)


def place_of(member, band, group, near):
    q = order(member, near)
    return jnp.where(band % 2 == 0, q, group - 1 - q)


def shared_place():
    group, near = lax.axis_size(GROUP), lax.axis_size("sub")
    me, band = lax.axis_index(GROUP), lax.axis_index("row")
    return lambda k: place_of(me ^ k, band, group, near)


def chunk_start(place, cuts, chunk):
    start = sum(cuts[:chunk])
    return jnp.where(place % 2 == 0, start, sum(cuts) - start - cuts[chunk])


def pack_kernel(chunk, cuts, left, right, image, *refs):
    group = lax.axis_size(GROUP)
    outs, image_s, sems, image_sem = refs[-group - 3 : -3], *refs[-3:]
    tile = image.shape[2]
    rows, lines = sum(cuts), cuts[chunk] * tile
    share = shared_place()
    copies = []

    def send(source, target):
        copy = pltpu.make_async_copy(source, target, sems.at[len(copies)])
        copy.start()
        copies.append(copy)

    if chunk == 0:
        colours = pltpu.make_async_copy(image, image_s, image_sem)
        colours.start()
    for k in range(group):
        first = share(k) * rows + chunk_start(share(k), cuts, chunk)
        first = pl.multiple_of(first * tile, tile)
        for s, side in enumerate((left, right)):
            send(side.at[pl.ds(first, lines), :], outs[k].at[pl.ds(s * lines, lines), :])
    if chunk == 0:
        count = strip_lines(rows)
        colours.wait()
        for k in range(group):
            start = pl.multiple_of(share(k) * rows, rows)
            strip = [image_s[ch, pl.ds(start, rows), :] for ch in range(3)]
            if count > 3 * rows:
                strip.append(jnp.zeros((count - 3 * rows, tile), F32))
            strip = jnp.concatenate(strip, axis=0)
            strip = jnp.concatenate([strip, jnp.zeros((count, C - tile), F32)], axis=1)
            outs[k][2 * lines : 2 * lines + count, :] = strip.astype(BF16)
    for copy in copies:
        copy.wait()


def pack(left, right, image, chunk, cuts, after=()):
    height, tile, _ = left.shape
    group = lax.axis_size(GROUP)
    count = strip_lines(sum(cuts))
    size = 2 * cuts[chunk] * tile + (count if chunk == 0 else 0)
    vmem = pl.BlockSpec(memory_space=pltpu.VMEM)
    hbm = pl.BlockSpec(memory_space=pltpu.HBM)
    return pl.pallas_call(
        functools.partial(pack_kernel, chunk, cuts),
        name="pack",
        out_shape=[jax.ShapeDtypeStruct((size, C), BF16)] * group,
        in_specs=[hbm] * 3 + [vmem] * len(after),
        out_specs=[vmem] * group,
        scratch_shapes=[
            pltpu.VMEM(image.shape, F32),
            pltpu.SemaphoreType.DMA((2 * group,)),
            pltpu.SemaphoreType.DMA,
        ],
        compiler_params=pltpu.CompilerParams(vmem_limit_bytes=(16 if after else 60) << 20),
    )(left.reshape(height * tile, C), right.reshape(height * tile, C), image, *after)


def weight_kernel(qk, value, out, occ, first, middle, last, *outs):
    q_t, v_t, o_t, occ_t, w1, w2, w3, w4, w5 = outs

    def flip(x):
        return jnp.transpose(x.astype(F32)).astype(BF16)

    q_t[...], v_t[...], o_t[...] = flip(qk[...]), flip(value[...]), flip(out[...])
    occ_t[...] = jnp.transpose(jnp.broadcast_to(occ[...], (C, C)))[:, :1]
    for a in range(3):
        block = []
        for b in range(3):
            block.append(first[3 * a + b].astype(F32))
            block.append(jnp.zeros((SLOTS - first.shape[1], CONV), F32))
        block.append(jnp.zeros((C - 3 * SLOTS, CONV), F32))
        block = jnp.concatenate(block, axis=0)
        block = jnp.concatenate([block, jnp.zeros((C, C - CONV), F32)], axis=1)
        w1[CONV * a : CONV * (a + 1), :] = jnp.transpose(block)[:CONV, : 4 * SLOTS].astype(BF16)
        for n, w in enumerate((w2, w3, w4)):
            taps = [middle[9 * n + 3 * a + b] for b in range(3)]
            w[CONV * a : CONV * (a + 1), :] = jnp.concatenate(taps, axis=1)
        taps = jnp.concatenate([last[3 * a + b].astype(F32) for b in range(3)], axis=1)
        taps = jnp.concatenate([taps, jnp.zeros((SLOTS - 2, 3 * CONV), F32)], axis=0)
        rest = taps if a == 0 else jnp.concatenate([rest, taps], axis=0)
    w5[...] = rest.astype(BF16)


def prepare_weights(qk, value, out, occ, first, middle, last):
    vmem = pl.BlockSpec(memory_space=pltpu.VMEM)
    square = jax.ShapeDtypeStruct((C, C), BF16)
    deep = jax.ShapeDtypeStruct((3 * CONV, 3 * CONV), BF16)
    results = pl.pallas_call(
        weight_kernel,
        name="weights",
        out_shape=[
            square,
            square,
            square,
            jax.ShapeDtypeStruct((C, 1), F32),
            jax.ShapeDtypeStruct((3 * CONV, 4 * SLOTS), BF16),
            deep,
            deep,
            deep,
            jax.ShapeDtypeStruct((3 * SLOTS, 3 * CONV), BF16),
        ],
        in_specs=[vmem] * 7,
        out_specs=[vmem] * 9,
        compiler_params=pltpu.CompilerParams(vmem_limit_bytes=16 << 20),
    )(
        qk,
        value,
        out,
        occ[None],
        first.transpose(0, 2, 1),
        middle.reshape(27, CONV, CONV),
        last,
    )
    q_t, v_t, o_t, occ_t, *convs = results
    return (q_t, qk, v_t, o_t, occ_t), tuple(convs)


def attention_kernel(cuts, chunk, *refs):
    group = lax.axis_size(GROUP)
    pieces, (qw, kw, vw, ow, occ) = refs[:group], refs[group : group + 5]
    earlier, (stacked_ref, maps_ref, left_s, right_s) = refs[group + 5 : -4], refs[-4:]
    count, length, _ = left_s.shape
    tile = length // group
    rows = sum(cuts)
    me, place = lax.axis_index(GROUP), shared_place()(0)
    for n in range(count):
        for k in range(group):
            start = pl.multiple_of((me ^ k) * tile, tile)
            left_s[n, pl.ds(start, tile), :] = pieces[k][n * tile : (n + 1) * tile]
            line = (count + n) * tile
            right_s[n, pl.ds(start, tile), :] = pieces[k][line : line + tile]
    slot = lax.broadcasted_iota(jnp.int32, (SLOTS, 1), 0)
    if chunk:
        stacked_ref[...] = earlier[0][...]
        maps_ref[...] = earlier[1][...]
    else:
        line = 2 * count * tile
        strips = [p[line : line + strip_lines(rows), :tile].astype(F32) for p in pieces]
        width = 1
        while width < group:
            high = (me & width) != 0
            strips = [
                jnp.where(
                    high,
                    jnp.concatenate([strips[n + 1], strips[n]], axis=1),
                    jnp.concatenate([strips[n], strips[n + 1]], axis=1),
                )
                for n in range(0, len(strips), 2)
            ]
            width *= 2
        zero = jnp.zeros((1, length), F32)
        for r in range(rows):
            colours = [strips[0][ch * rows + r : ch * rows + r + 1] for ch in range(3)]
            stacked_ref[r] = jnp.concatenate(
                [zero, zero] + colours + [zero] * (SLOTS - 5), axis=0
            ).astype(BF16)
        maps_ref[...] = jnp.zeros_like(maps_ref)
    first = chunk_start(place, cuts, chunk)
    for n in range(count):
        disparity, occlusion = attention_row(
            left_s[n], right_s[n], qw[...], kw[...], vw[...], ow[...], occ[...]
        )
        r = first + n
        maps_ref[r] = jnp.concatenate([disparity, occlusion], axis=0)
        full = jnp.where(slot == 0, disparity, stacked_ref[r].astype(F32))
        stacked_ref[r] = jnp.where(slot == 1, occlusion, full).astype(BF16)


def attention(pieces, weights, earlier, cuts, chunk, length):
    rows, count = sum(cuts), cuts[chunk]
    vmem = pl.BlockSpec(memory_space=pltpu.VMEM)
    pairs = count * HEADS * length * length
    return pl.pallas_call(
        functools.partial(attention_kernel, cuts, chunk),
        name="attention",
        out_shape=(
            jax.ShapeDtypeStruct((rows, SLOTS, length), BF16),
            jax.ShapeDtypeStruct((rows, 2, length), F32),
        ),
        in_specs=[vmem] * (len(pieces) + len(weights) + len(earlier)),
        out_specs=(vmem, vmem),
        scratch_shapes=[pltpu.VMEM((count, length, C), BF16)] * 2,
        compiler_params=pltpu.CompilerParams(vmem_limit_bytes=24 << 20),
        cost_estimate=pl.CostEstimate(
            flops=pairs * 4 * C, transcendentals=pairs, bytes_accessed=8 * count * length * C
        ),
    )(*pieces, *weights, *earlier)


def spread_taps(x):
    length = x.shape[1]
    column = lax.broadcasted_iota(jnp.int32, (1, length), 1)
    before = jnp.where(column == 0, 0.0, pltpu.roll(x, 1, 1))
    after = jnp.where(column == length - 1, 0.0, pltpu.roll(x, length - 1, 1))
    return before, x, after


def conv_rows(source, weight, outs, count, finish):
    def at(q):
        p = dot(weight[...], source[q], ((1,), (0,)))
        return p[:outs], p[outs : 2 * outs], p[2 * outs :]

    top0, top1, _ = at(0)
    next0, next1, _ = at(1)
    del top1

    def body(r, carry):
        first, second = carry
        p0, p1, p2 = at(r + 2)
        finish(r, first + p2)
        return second + p1, p0

    carry = (top0 + next1, next0)
    for r in range(count):
        carry = body(r, carry)


def conv_kernel(group, hops, own, maps, *refs):
    others = refs[: 2 * hops]
    w1, w2, w3, w4, w5 = refs[2 * hops : 2 * hops + 5]
    outs = refs[2 * hops + 5 : 2 * hops + 5 + group]
    x0, x1, x2, x3, x4 = refs[2 * hops + 5 + group :]
    rows, _, length = own.shape
    me = lax.axis_index(GROUP)
    place = lax.axis_index("row") * group + shared_place()(0)
    last = lax.axis_size(BANDS) * rows
    base = place * rows

    def put(q, block):
        before, same, after = spread_taps(block.astype(F32))
        zero = jnp.zeros_like(same)
        x0[q] = jnp.concatenate([before, same, after, zero], axis=0).astype(BF16)

    for q in range(rows):
        put(RIM + q, own[q])
    for d in range(1, hops + 1):
        flag = jnp.bitwise_and(place, d) != 0
        a, b = others[2 * d - 2], others[2 * d - 1]
        for q in range(rows):
            up = RIM - d * rows + q
            if up >= 0:
                inside = base - d * rows >= 0
                put(up, jnp.where(inside, jnp.where(flag, a[q], b[q]).astype(F32), 0.0))
            down = RIM + d * rows + q
            if down < rows + 2 * RIM:
                inside = base + d * rows < last
                put(down, jnp.where(inside, jnp.where(flag, b[q], a[q]).astype(F32), 0.0))

    def store(target, lead, residual=None):
        def finish(r, total):
            if residual is not None:
                total = total + residual[r + 2, CONV : 2 * CONV].astype(F32)
            g = base + r - lead
            inside = jnp.logical_and(g >= 0, g < last)
            y = jnp.where(inside, jnp.maximum(total, 0.0), 0.0)
            before, same, after = spread_taps(y)
            target[r, :CONV] = before.astype(BF16)
            target[r, CONV : 2 * CONV] = same.astype(BF16)
            target[r, 2 * CONV :] = after.astype(BF16)

        return finish

    conv_rows(x0, w1, CONV, rows + 8, store(x1, 4))
    conv_rows(x1, w2, CONV, rows + 6, store(x2, 3))
    conv_rows(x2, w3, CONV, rows + 4, store(x3, 2, x1))
    conv_rows(x3, w4, CONV, rows + 2, store(x4, 1))

    tile = length // group

    def last_row(r, total):
        m = maps[r]
        disparity = m[:1] + total[:1]
        occlusion = jax.nn.sigmoid(m[1:2] + total[1:2])
        finals[0].append(disparity)
        finals[1].append(occlusion)

    finals = [], []
    conv_rows(x4, w5, SLOTS, rows, last_row)
    for n in range(2):
        both = jnp.concatenate(finals[n], axis=0)
        cut = [both[:, tile * c : tile * (c + 1)] for c in range(group)]
        for k in range(group):
            pick = cut[0]
            for c in range(1, group):
                pick = jnp.where((me ^ k) == c, cut[c], pick)
            outs[k][n] = pick


def convolutions(own, maps, others, weights, group):
    rows, _, length = own.shape
    tile = length // group
    hops = len(others) // 2
    vmem = pl.BlockSpec(memory_space=pltpu.VMEM)
    depth = 3 * CONV
    return pl.pallas_call(
        functools.partial(conv_kernel, group, hops),
        name="convolutions",
        out_shape=[jax.ShapeDtypeStruct((2, rows, tile), F32)] * group,
        in_specs=[vmem] * (2 + len(others) + len(weights)),
        out_specs=[vmem] * group,
        scratch_shapes=[
            pltpu.VMEM((rows + 10, 4 * SLOTS, length), BF16),
            pltpu.VMEM((rows + 8, depth, length), BF16),
            pltpu.VMEM((rows + 6, depth, length), BF16),
            pltpu.VMEM((rows + 4, depth, length), BF16),
            pltpu.VMEM((rows + 2, depth, length), BF16),
        ],
        compiler_params=pltpu.CompilerParams(vmem_limit_bytes=40 << 20),
    )(own, maps, *others, *weights)


def place_kernel(group, *refs):
    pieces, outs = refs[:group], refs[group:]
    rows = pieces[0].shape[1]
    share = shared_place()
    for k in range(group):
        start = pl.multiple_of(share(k) * rows, rows)
        for n in range(2):
            outs[n][pl.ds(start, rows), :] = pieces[k][n]


def place_rows(pieces):
    group = len(pieces)
    _, rows, tile = pieces[0].shape
    vmem = pl.BlockSpec(memory_space=pltpu.VMEM)
    return pl.pallas_call(
        functools.partial(place_kernel, group),
        name="place",
        out_shape=[jax.ShapeDtypeStruct((rows * group, tile), F32)] * 2,
        in_specs=[vmem] * group,
        out_specs=[vmem] * 2,
        compiler_params=pltpu.CompilerParams(vmem_limit_bytes=4 << 20),
    )(*pieces)


def swap(x, k):
    count = lax.axis_size(GROUP)
    return lax.ppermute(x, GROUP, [(i, i ^ k) for i in range(count)])


def neighbours(x, d, odd):
    count, group, near = lax.axis_size(BANDS), lax.axis_size(GROUP), lax.axis_size("sub")

    def device(place):
        band, q = divmod(place, group)
        chip, core = divmod(q if band % 2 == 0 else group - 1 - q, near)
        return band * group + chip * near + (core if chip % 2 == 0 else near - 1 - core)

    pairs = [(i, ((i + d) ^ d) - d if odd else i ^ d) for i in range(count)]
    parts = lax.axis_size("grp")
    targets = []
    for part in range(parts):
        for i, j in pairs:
            at = part
            if not 0 <= j < count:
                at, j = (part ^ 1 if part ^ 1 < parts else part), i
            targets.append((part * count + device(i), at * count + device(j)))
    return lax.ppermute(x, ("grp",) + BANDS, targets)


def chunks_of(rows):
    ends = 3 * rows // 8
    return tuple(c for c in (ends, rows - 2 * ends, ends) if c)


def per_device(
    left_features,
    right_features,
    left_image,
    query_key,
    value_weight,
    out_weight,
    occlusion_weight,
    first_conv,
    middle_conv,
    last_conv,
):
    height, tile, _ = left_features.shape
    group = lax.axis_size(GROUP)
    rows = height // group
    length = tile * group
    cuts = chunks_of(rows)
    features = (left_features, right_features, left_image)
    packed = pack(*features, 0, cuts)
    tables = (
        query_key,
        value_weight,
        out_weight,
        occlusion_weight,
        first_conv,
        middle_conv,
        last_conv,
    )
    packed, tables = lax.optimization_barrier((packed, tables))
    pieces = []
    for c in range(len(cuts)):
        if c:
            packed = pack(*features, c, cuts, (pieces[-1][1],))
        pieces.append([packed[0]] + [swap(packed[k], k) for k in range(1, group)])

    weights, convs = prepare_weights(*tables)
    weights, convs = lax.optimization_barrier((weights, convs))
    done = ()
    others = []
    hops = -(-RIM // rows)
    for c in range(len(cuts)):
        done = attention(pieces[c], weights, done, cuts, c, length)
        if hops == 1 and len(others) == 0 and sum(cuts[: c + 1]) >= RIM:
            others = [neighbours(done[0], 1, True)]
    stacked, maps = done
    if hops == 1:
        others = [neighbours(stacked, 1, False)] + others
    else:
        for d in range(1, hops + 1):
            others += [neighbours(stacked, d, odd) for odd in (False, True)]
    results = convolutions(stacked, maps, others, convs, group)
    results = [results[0]] + [swap(results[k], k) for k in range(1, group)]
    return tuple(place_rows(results))


def solution(mesh):
    tiles = P(("grp", "row"), ("col", "sub"))
    placed = (
        P(("grp", "row"), ("col", "sub"), None),
        P(("grp", "row"), ("col", "sub"), None),
        P(None, ("grp", "row"), ("col", "sub")),
    ) + (P(),) * 7
    return jax.shard_map(
        per_device, mesh=mesh, in_specs=placed, out_specs=(tiles, tiles), check_vma=False
    )
```

```python
import functools

import jax
import jax.numpy as jnp
from jax import lax
from jax.experimental import pallas as pl
from jax.experimental.pallas import tpu as pltpu
from jax.sharding import PartitionSpec as P

C = 128
HEADS = 8
HEAD = 16
CONV = 64
RIM = 5
SLOTS = 8
BLOCK = 128
F32 = jnp.float32
BF16 = jnp.bfloat16
GROUP = ("col", "sub")
BANDS = ("row", "col", "sub")


def dot(a, b, dims):
    return lax.dot_general(a, b, (dims, ((), ())), preferred_element_type=F32)


def score_blocks(queries, keys):
    channel = lax.broadcasted_iota(jnp.int32, (1, C), 1)
    found = []
    for j in range(keys.shape[0] // BLOCK):
        part = keys[BLOCK * j : BLOCK * (j + 1)]
        by_head = [
            jnp.where(channel // HEAD == h, part, jnp.zeros_like(part)) for h in range(HEADS)
        ]
        s = dot(jnp.concatenate(by_head, axis=0), queries[:, BLOCK * j :], ((1,), (0,)))
        found.append([s[:, i : i + BLOCK] for i in range(0, s.shape[1], BLOCK)])
    return found


def attention_row(left, right, qw, kw, vw, ow, occ):
    length = left.shape[0]
    blocks = length // BLOCK
    queries = (dot(qw, left, ((1,), (1,))) * (HEAD**-0.5)).astype(BF16)
    keys = dot(right, kw, ((1,), (0,))).astype(BF16)
    values = dot(vw, right, ((1,), (1,))).astype(BF16)
    scores = score_blocks(queries, keys)

    key_at = lax.broadcasted_iota(jnp.int32, (BLOCK, BLOCK), 0)
    query_at = lax.broadcasted_iota(jnp.int32, (BLOCK, BLOCK), 1)
    allowed = key_at <= query_at
    line = lax.broadcasted_iota(jnp.int32, (HEAD, length), 0)
    place = lax.broadcasted_iota(jnp.int32, (HEAD, length), 1)
    counts = jnp.where(
        line == 0,
        1,
        jnp.where(line == 1, place % BLOCK, jnp.where(line == 2, place - place % BLOCK, 0)),
    )
    counts = counts.astype(F32).astype(BF16)

    heads = [[] for _ in range(blocks)]
    means = [jnp.zeros((1, BLOCK), F32) for _ in range(blocks)]
    for h in range(0, HEADS, 2):
        stacked = jnp.concatenate([values[HEAD * h : HEAD * (h + 2)], counts], axis=0)
        for i in range(blocks):
            expon = []
            for g in (h, h + 1):
                parts = [scores[j][i - j][BLOCK * g : BLOCK * (g + 1)] for j in range(i + 1)]
                parts[i] = jnp.where(allowed, parts[i], -jnp.inf)
                largest = functools.reduce(
                    jnp.maximum, [jnp.max(p, axis=0, keepdims=True) for p in parts]
                )
                expon.append(
                    jnp.concatenate([jnp.exp(p - largest).astype(BF16) for p in parts], axis=0)
                )
            sums = dot(
                stacked[:, : BLOCK * (i + 1)], jnp.concatenate(expon, axis=1), ((1,), (0,))
            )
            for g in range(2):
                part = sums[:, BLOCK * g : BLOCK * (g + 1)]
                inverse = 1.0 / part[2 * HEAD : 2 * HEAD + 1]
                heads[i].append((part[HEAD * g : HEAD * (g + 1)] * inverse).astype(BF16))
                total = part[2 * HEAD + 1 : 2 * HEAD + 2] + part[2 * HEAD + 2 : 2 * HEAD + 3]
                means[i] = means[i] + total * inverse

    head_out = jnp.concatenate([jnp.concatenate(b, axis=0) for b in heads], axis=1)
    mean = jnp.concatenate(means, axis=1)
    column = lax.broadcasted_iota(jnp.int32, (1, length), 1).astype(F32)
    disparity = (HEADS * column - mean) * (8.0 / (HEADS * length))
    attended = dot(ow, head_out, ((1,), (0,)))
    centred = attended - jnp.mean(attended, axis=0, keepdims=True)
    spread = jnp.mean(centred * centred, axis=0, keepdims=True)
    occlusion = jnp.sum(centred * occ, axis=0, keepdims=True) * lax.rsqrt(spread + 1e-05)
    return disparity, occlusion


def strip_lines(rows):
    return -(-3 * rows // 16) * 16


def order(k, near):
    chip, core = k // near, k % near
    return chip * near + jnp.where(chip % 2 == 0, core, near - 1 - core)


def place_of(member, band, group, near):
    q = order(member, near)
    return jnp.where(band % 2 == 0, q, group - 1 - q)


def shared_place():
    group, near = lax.axis_size(GROUP), lax.axis_size("sub")
    me, band = lax.axis_index(GROUP), lax.axis_index("row")
    return lambda k: place_of(me ^ k, band, group, near)


def chunk_start(place, cuts, chunk):
    start = sum(cuts[:chunk])
    return jnp.where(place % 2 == 0, start, sum(cuts) - start - cuts[chunk])


def pack_kernel(chunk, cuts, left, right, image, *refs):
    group = lax.axis_size(GROUP)
    outs, image_s, sems, image_sem = refs[-group - 3 : -3], *refs[-3:]
    tile = image.shape[2]
    rows, lines = sum(cuts), cuts[chunk] * tile
    share = shared_place()
    copies = []

    def send(source, target):
        copy = pltpu.make_async_copy(source, target, sems.at[len(copies)])
        copy.start()
        copies.append(copy)

    if chunk == 0:
        colours = pltpu.make_async_copy(image, image_s, image_sem)
        colours.start()
    for k in range(group):
        first = share(k) * rows + chunk_start(share(k), cuts, chunk)
        first = pl.multiple_of(first * tile, tile)
        for s, side in enumerate((left, right)):
            send(side.at[pl.ds(first, lines), :], outs[k].at[pl.ds(s * lines, lines), :])
    if chunk == 0:
        count = strip_lines(rows)
        colours.wait()
        for k in range(group):
            start = pl.multiple_of(share(k) * rows, rows)
            strip = [image_s[ch, pl.ds(start, rows), :] for ch in range(3)]
            if count > 3 * rows:
                strip.append(jnp.zeros((count - 3 * rows, tile), F32))
            strip = jnp.concatenate(strip, axis=0)
            strip = jnp.concatenate([strip, jnp.zeros((count, C - tile), F32)], axis=1)
            outs[k][2 * lines : 2 * lines + count, :] = strip.astype(BF16)
    for copy in copies:
        copy.wait()


def pack(left, right, image, chunk, cuts, after=()):
    height, tile, _ = left.shape
    group = lax.axis_size(GROUP)
    count = strip_lines(sum(cuts))
    size = 2 * cuts[chunk] * tile + (count if chunk == 0 else 0)
    vmem = pl.BlockSpec(memory_space=pltpu.VMEM)
    hbm = pl.BlockSpec(memory_space=pltpu.HBM)
    return pl.pallas_call(
        functools.partial(pack_kernel, chunk, cuts),
        name="pack",
        out_shape=[jax.ShapeDtypeStruct((size, C), BF16)] * group,
        in_specs=[hbm] * 3 + [vmem] * len(after),
        out_specs=[vmem] * group,
        scratch_shapes=[
            pltpu.VMEM(image.shape, F32),
            pltpu.SemaphoreType.DMA((2 * group,)),
            pltpu.SemaphoreType.DMA,
        ],
        compiler_params=pltpu.CompilerParams(vmem_limit_bytes=(16 if after else 60) << 20),
    )(left.reshape(height * tile, C), right.reshape(height * tile, C), image, *after)


def weight_kernel(qk, value, out, occ, first, middle, last, *outs):
    q_t, v_t, o_t, occ_t, w1, w2, w3, w4, w5 = outs

    def flip(x):
        return jnp.transpose(x.astype(F32)).astype(BF16)

    q_t[...], v_t[...], o_t[...] = flip(qk[...]), flip(value[...]), flip(out[...])
    occ_t[...] = jnp.transpose(jnp.broadcast_to(occ[...], (C, C)))[:, :1]
    for a in range(3):
        block = []
        for b in range(3):
            block.append(first[3 * a + b].astype(F32))
            block.append(jnp.zeros((SLOTS - first.shape[1], CONV), F32))
        block.append(jnp.zeros((C - 3 * SLOTS, CONV), F32))
        block = jnp.concatenate(block, axis=0)
        block = jnp.concatenate([block, jnp.zeros((C, C - CONV), F32)], axis=1)
        w1[CONV * a : CONV * (a + 1), :] = jnp.transpose(block)[:CONV, : 4 * SLOTS].astype(BF16)
        for n, w in enumerate((w2, w3, w4)):
            taps = [middle[9 * n + 3 * a + b] for b in range(3)]
            w[CONV * a : CONV * (a + 1), :] = jnp.concatenate(taps, axis=1)
        taps = jnp.concatenate([last[3 * a + b].astype(F32) for b in range(3)], axis=1)
        taps = jnp.concatenate([taps, jnp.zeros((SLOTS - 2, 3 * CONV), F32)], axis=0)
        rest = taps if a == 0 else jnp.concatenate([rest, taps], axis=0)
    w5[...] = rest.astype(BF16)


def prepare_weights(qk, value, out, occ, first, middle, last):
    vmem = pl.BlockSpec(memory_space=pltpu.VMEM)
    square = jax.ShapeDtypeStruct((C, C), BF16)
    deep = jax.ShapeDtypeStruct((3 * CONV, 3 * CONV), BF16)
    results = pl.pallas_call(
        weight_kernel,
        name="weights",
        out_shape=[
            square,
            square,
            square,
            jax.ShapeDtypeStruct((C, 1), F32),
            jax.ShapeDtypeStruct((3 * CONV, 4 * SLOTS), BF16),
            deep,
            deep,
            deep,
            jax.ShapeDtypeStruct((3 * SLOTS, 3 * CONV), BF16),
        ],
        in_specs=[vmem] * 7,
        out_specs=[vmem] * 9,
        compiler_params=pltpu.CompilerParams(vmem_limit_bytes=16 << 20),
    )(
        qk,
        value,
        out,
        occ[None],
        first.transpose(0, 2, 1),
        middle.reshape(27, CONV, CONV),
        last,
    )
    q_t, v_t, o_t, occ_t, *convs = results
    return (q_t, qk, v_t, o_t, occ_t), tuple(convs)


def attention_kernel(cuts, chunk, *refs):
    group = lax.axis_size(GROUP)
    pieces, (qw, kw, vw, ow, occ) = refs[:group], refs[group : group + 5]
    earlier, (stacked_ref, maps_ref, left_s, right_s) = refs[group + 5 : -4], refs[-4:]
    count, length, _ = left_s.shape
    tile = length // group
    rows = sum(cuts)
    me, place = lax.axis_index(GROUP), shared_place()(0)
    for n in range(count):
        for k in range(group):
            start = pl.multiple_of((me ^ k) * tile, tile)
            left_s[n, pl.ds(start, tile), :] = pieces[k][n * tile : (n + 1) * tile]
            line = (count + n) * tile
            right_s[n, pl.ds(start, tile), :] = pieces[k][line : line + tile]
    slot = lax.broadcasted_iota(jnp.int32, (SLOTS, 1), 0)
    if chunk:
        stacked_ref[...] = earlier[0][...]
        maps_ref[...] = earlier[1][...]
    else:
        line = 2 * count * tile
        strips = [p[line : line + strip_lines(rows), :tile].astype(F32) for p in pieces]
        width = 1
        while width < group:
            high = (me & width) != 0
            strips = [
                jnp.where(
                    high,
                    jnp.concatenate([strips[n + 1], strips[n]], axis=1),
                    jnp.concatenate([strips[n], strips[n + 1]], axis=1),
                )
                for n in range(0, len(strips), 2)
            ]
            width *= 2
        zero = jnp.zeros((1, length), F32)
        for r in range(rows):
            colours = [strips[0][ch * rows + r : ch * rows + r + 1] for ch in range(3)]
            stacked_ref[r] = jnp.concatenate(
                [zero, zero] + colours + [zero] * (SLOTS - 5), axis=0
            ).astype(BF16)
        maps_ref[...] = jnp.zeros_like(maps_ref)
    first = chunk_start(place, cuts, chunk)
    for n in range(count):
        disparity, occlusion = attention_row(
            left_s[n], right_s[n], qw[...], kw[...], vw[...], ow[...], occ[...]
        )
        r = first + n
        maps_ref[r] = jnp.concatenate([disparity, occlusion], axis=0)
        full = jnp.where(slot == 0, disparity, stacked_ref[r].astype(F32))
        stacked_ref[r] = jnp.where(slot == 1, occlusion, full).astype(BF16)


def attention(pieces, weights, earlier, cuts, chunk, length):
    rows, count = sum(cuts), cuts[chunk]
    vmem = pl.BlockSpec(memory_space=pltpu.VMEM)
    pairs = count * HEADS * length * length
    return pl.pallas_call(
        functools.partial(attention_kernel, cuts, chunk),
        name="attention",
        out_shape=(
            jax.ShapeDtypeStruct((rows, SLOTS, length), BF16),
            jax.ShapeDtypeStruct((rows, 2, length), F32),
        ),
        in_specs=[vmem] * (len(pieces) + len(weights) + len(earlier)),
        out_specs=(vmem, vmem),
        scratch_shapes=[pltpu.VMEM((count, length, C), BF16)] * 2,
        compiler_params=pltpu.CompilerParams(vmem_limit_bytes=24 << 20),
        cost_estimate=pl.CostEstimate(
            flops=pairs * 4 * C, transcendentals=pairs, bytes_accessed=8 * count * length * C
        ),
    )(*pieces, *weights, *earlier)


def spread_taps(x):
    length = x.shape[1]
    column = lax.broadcasted_iota(jnp.int32, (1, length), 1)
    zero = jnp.zeros_like(x)
    before = jnp.where(column == 0, zero, pltpu.roll(x, 1, 1))
    after = jnp.where(column == length - 1, zero, pltpu.roll(x, length - 1, 1))
    return before, x, after


def conv_rows(source, weight, outs, count, finish):
    def at(q):
        p = dot(weight[...], source[q], ((1,), (0,)))
        return p[:outs], p[outs : 2 * outs], p[2 * outs :]

    top0, top1, _ = at(0)
    next0, next1, _ = at(1)
    del top1

    def body(r, carry):
        first, second = carry
        p0, p1, p2 = at(r + 2)
        finish(r, first + p2)
        return second + p1, p0

    carry = (top0 + next1, next0)
    for r in range(count):
        carry = body(r, carry)


def conv_kernel(group, hops, own, maps, *refs):
    others = refs[: 2 * hops]
    w1, w2, w3, w4, w5 = refs[2 * hops : 2 * hops + 5]
    outs = refs[2 * hops + 5 : 2 * hops + 5 + group]
    x0, x1, x2, x3, x4 = refs[2 * hops + 5 + group :]
    rows, _, length = own.shape
    me = lax.axis_index(GROUP)
    place = lax.axis_index("row") * group + shared_place()(0)
    last = lax.axis_size(BANDS) * rows
    base = place * rows

    def put(q, block):
        before, same, after = spread_taps(block.astype(F32))
        zero = jnp.zeros_like(same)
        x0[q] = jnp.concatenate([before, same, after, zero], axis=0).astype(BF16)

    for q in range(rows):
        put(RIM + q, own[q])
    for d in range(1, hops + 1):
        flag = jnp.bitwise_and(place, d) != 0
        a, b = others[2 * d - 2], others[2 * d - 1]
        for q in range(rows):
            up = RIM - d * rows + q
            if up >= 0:
                inside = base - d * rows >= 0
                put(up, jnp.where(inside, jnp.where(flag, a[q], b[q]).astype(F32), 0.0))
            down = RIM + d * rows + q
            if down < rows + 2 * RIM:
                inside = base + d * rows < last
                put(down, jnp.where(inside, jnp.where(flag, b[q], a[q]).astype(F32), 0.0))

    def store(target, lead, residual=None):
        def finish(r, total):
            if residual is not None:
                total = total + residual[r + 2, CONV : 2 * CONV].astype(F32)
            g = base + r - lead
            inside = jnp.logical_and(g >= 0, g < last)
            y = jnp.where(inside, jnp.maximum(total, 0.0), 0.0)
            before, same, after = spread_taps(y.astype(BF16))
            target[r, :CONV] = before
            target[r, CONV : 2 * CONV] = same
            target[r, 2 * CONV :] = after

        return finish

    conv_rows(x0, w1, CONV, rows + 8, store(x1, 4))
    conv_rows(x1, w2, CONV, rows + 6, store(x2, 3))
    conv_rows(x2, w3, CONV, rows + 4, store(x3, 2, x1))
    conv_rows(x3, w4, CONV, rows + 2, store(x4, 1))

    tile = length // group

    def last_row(r, total):
        m = maps[r]
        disparity = m[:1] + total[:1]
        occlusion = jax.nn.sigmoid(m[1:2] + total[1:2])
        finals[0].append(disparity)
        finals[1].append(occlusion)

    finals = [], []
    conv_rows(x4, w5, SLOTS, rows, last_row)
    for n in range(2):
        both = jnp.concatenate(finals[n], axis=0)
        cut = [both[:, tile * c : tile * (c + 1)] for c in range(group)]
        for k in range(group):
            pick = cut[0]
            for c in range(1, group):
                pick = jnp.where((me ^ k) == c, cut[c], pick)
            outs[k][n] = pick


def convolutions(own, maps, others, weights, group):
    rows, _, length = own.shape
    tile = length // group
    hops = len(others) // 2
    vmem = pl.BlockSpec(memory_space=pltpu.VMEM)
    depth = 3 * CONV
    return pl.pallas_call(
        functools.partial(conv_kernel, group, hops),
        name="convolutions",
        out_shape=[jax.ShapeDtypeStruct((2, rows, tile), F32)] * group,
        in_specs=[vmem] * (2 + len(others) + len(weights)),
        out_specs=[vmem] * group,
        scratch_shapes=[
            pltpu.VMEM((rows + 10, 4 * SLOTS, length), BF16),
            pltpu.VMEM((rows + 8, depth, length), BF16),
            pltpu.VMEM((rows + 6, depth, length), BF16),
            pltpu.VMEM((rows + 4, depth, length), BF16),
            pltpu.VMEM((rows + 2, depth, length), BF16),
        ],
        compiler_params=pltpu.CompilerParams(vmem_limit_bytes=40 << 20),
    )(own, maps, *others, *weights)


def place_kernel(group, *refs):
    pieces, outs = refs[:group], refs[group:]
    rows = pieces[0].shape[1]
    share = shared_place()
    for k in range(group):
        start = pl.multiple_of(share(k) * rows, rows)
        for n in range(2):
            outs[n][pl.ds(start, rows), :] = pieces[k][n]


def place_rows(pieces):
    group = len(pieces)
    _, rows, tile = pieces[0].shape
    vmem = pl.BlockSpec(memory_space=pltpu.VMEM)
    return pl.pallas_call(
        functools.partial(place_kernel, group),
        name="place",
        out_shape=[jax.ShapeDtypeStruct((rows * group, tile), F32)] * 2,
        in_specs=[vmem] * group,
        out_specs=[vmem] * 2,
        compiler_params=pltpu.CompilerParams(vmem_limit_bytes=4 << 20),
    )(*pieces)


def swap(x, k):
    count = lax.axis_size(GROUP)
    return lax.ppermute(x, GROUP, [(i, i ^ k) for i in range(count)])


def neighbours(x, d, odd):
    count, group, near = lax.axis_size(BANDS), lax.axis_size(GROUP), lax.axis_size("sub")

    def device(place):
        band, q = divmod(place, group)
        chip, core = divmod(q if band % 2 == 0 else group - 1 - q, near)
        return band * group + chip * near + (core if chip % 2 == 0 else near - 1 - core)

    pairs = [(i, ((i + d) ^ d) - d if odd else i ^ d) for i in range(count)]
    parts = lax.axis_size("grp")
    targets = []
    for part in range(parts):
        for i, j in pairs:
            at = part
            if not 0 <= j < count:
                at, j = (part ^ 1 if part ^ 1 < parts else part), i
            targets.append((part * count + device(i), at * count + device(j)))
    return lax.ppermute(x, ("grp",) + BANDS, targets)


def chunks_of(rows):
    ends = 3 * rows // 8
    return tuple(c for c in (ends, rows - 2 * ends, ends) if c)


def per_device(
    left_features,
    right_features,
    left_image,
    query_key,
    value_weight,
    out_weight,
    occlusion_weight,
    first_conv,
    middle_conv,
    last_conv,
):
    height, tile, _ = left_features.shape
    group = lax.axis_size(GROUP)
    rows = height // group
    length = tile * group
    cuts = chunks_of(rows)
    features = (left_features, right_features, left_image)
    packed = pack(*features, 0, cuts)
    tables = (
        query_key,
        value_weight,
        out_weight,
        occlusion_weight,
        first_conv,
        middle_conv,
        last_conv,
    )
    packed, tables = lax.optimization_barrier((packed, tables))
    pieces = []
    for c in range(len(cuts)):
        if c:
            packed = pack(*features, c, cuts, (pieces[-1][1],))
        pieces.append([packed[0]] + [swap(packed[k], k) for k in range(1, group)])

    weights, convs = prepare_weights(*tables)
    weights, convs = lax.optimization_barrier((weights, convs))
    done = ()
    others = []
    hops = -(-RIM // rows)
    for c in range(len(cuts)):
        done = attention(pieces[c], weights, done, cuts, c, length)
        if hops == 1 and len(others) == 0 and sum(cuts[: c + 1]) >= RIM:
            others = [neighbours(done[0], 1, True)]
    stacked, maps = done
    if hops == 1:
        others = [neighbours(stacked, 1, False)] + others
    else:
        for d in range(1, hops + 1):
            others += [neighbours(stacked, d, odd) for odd in (False, True)]
    results = convolutions(stacked, maps, others, convs, group)
    results = [results[0]] + [swap(results[k], k) for k in range(1, group)]
    return tuple(place_rows(results))


def solution(mesh):
    tiles = P(("grp", "row"), ("col", "sub"))
    placed = (
        P(("grp", "row"), ("col", "sub"), None),
        P(("grp", "row"), ("col", "sub"), None),
        P(None, ("grp", "row"), ("col", "sub")),
    ) + (P(),) * 7
    return jax.shard_map(
        per_device, mesh=mesh, in_specs=placed, out_specs=(tiles, tiles), check_vma=False
    )
```
